256 devices in a mesh: facet: 16 (over z, core), row: 8 (over x_hi, y), sub: 2 (over x_lo).
Axes of the slice: x: 4 (x_hi: 2, x_lo: 2; x = x_hi * 2 + x_lo), y: 4, z: 8, core: 2. Of those that a mesh axis runs over, the one named last changes fastest.
Arguments:
- facet_model: bfloat16 [2, 4, 8192, 8192], P(None, 'sub', ('facet', 'row')), may hold values from -6 to 6
- sub_offsets: int32 [256], replicated, may hold values from 0 to 65535
- tile_rows: int32 [256, 4], P(('facet', 'row', 'sub')), may hold values from 0 to 120
- tile_counts: int32 [256], P(('facet', 'row', 'sub')), may hold values from 1 to 4, as said below
- visibilities: bfloat16 [256, 4, 32, 8, 256], P(('facet', 'row', 'sub')), may hold values from -6 to 6
Outputs:
- residual_facets: bfloat16 [2, 4, 8192, 8192], P(None, 'sub', ('facet', 'row'))
- residual_vis: bfloat16 [256, 4, 32, 8, 256], P(('facet', 'row', 'sub'))
The draws below stay inside these ranges and needn't reach their ends.
Inputs may be any that keep to these rules, and one draw needn't show every extreme that they name: tile_counts[s] tiles of subgrid s are live, the first ones; some subgrid has all 4 tiles live. Tile j of subgrid s covers subgrid rows tile_rows[s, j] to tile_rows[s, j] + 7; tiles may intersect.
All inputs are finite; a program needn't handle non-finite values.
Results may differ from the reference program's by a relative error of at most 0.014.
Values may be sent and summed in bfloat16 or wider, within the bound.
No kernel may reach another device: no remote copies, remote signals or barrier semaphores. Data moves between devices by JAX's collectives and lax.ppermute only.
A program may use at most 128 MiB of HBM per device.

```python
import math
import jax
import jax.numpy as jnp
from jax import lax

SKY = 65536
FP = 8192
CS = 64
SG = 128
TMAX = 4
CH = 32
TR = 8
NF = 4
SUBGRIDS = 256


def draw_tile_counts(key, part):
    counts = jax.random.randint(key, (SUBGRIDS,), 1, TMAX + 1)
    chosen = jax.random.randint(jax.random.fold_in(key, 7), (), 0, SUBGRIDS)
    return jnp.where(jnp.arange(SUBGRIDS) == chosen, TMAX, counts).astype(jnp.int32)


def with_ends(array, key, least, high):
    shape = array.shape
    place = [jax.random.randint(jax.random.fold_in(key, axis), (), 0, shape[axis]) for axis in range(len(shape))]
    array = array.at[tuple(place)].set(least)
    longest = shape.index(max(shape))
    place[longest] = (place[longest] + 1) % shape[longest]
    return array.at[tuple(place)].set(high)


def block_levels(rng, extent, split, low, high):
    factor_of = 1.0
    for position, blocks in split:
        steps = jax.random.uniform(jax.random.fold_in(jax.random.fold_in(rng, 6), position), (blocks,), jnp.float32, low / len(split), high / len(split))
        factor_of = factor_of * jnp.repeat(jnp.exp(steps), extent[position] // blocks).reshape((-1,) + (1,) * (len(extent) - 1 - position))
    return factor_of


def normal_values(rng, dims, scale, reach, cuts=(), held_as=jnp.bfloat16):
    drawn = scale * jax.random.normal(rng, dims, jnp.float32)
    if cuts:
        drawn = drawn * block_levels(rng, dims, cuts, -0.22, 0.18)
    return jnp.clip(drawn, -reach, reach).astype(held_as)


def setup_inputs(seed: int = 0) -> dict:
    seeds = jax.random.split(jax.random.key(seed), 6)
    facet_model = normal_values(seeds[0], (2, NF, FP, FP), 1.0, 6.0, ((1, 2), (2, 128)))
    sub_offsets = with_ends(jax.random.randint(seeds[1], (SUBGRIDS,), 0, SKY), jax.random.fold_in(seeds[1], 1), 0, SKY - 1).astype(jnp.int32)
    tile_rows = with_ends(jax.random.randint(seeds[2], (SUBGRIDS, TMAX), 0, SG - TR + 1), jax.random.fold_in(seeds[2], 1), 0, SG - TR).astype(jnp.int32)
    tile_counts = draw_tile_counts(jax.random.fold_in(seeds[5], 71), 0)
    visibilities = normal_values(seeds[4], (SUBGRIDS, TMAX, CH, TR, 2 * SG), 1.0, 6.0, ((0, 256),))
    return {"facet_model": facet_model, "sub_offsets": sub_offsets, "tile_rows": tile_rows, "tile_counts": tile_counts, "visibilities": visibilities}


two_pi = 2.0 * math.pi

def modmul(left, right, modulus):
    lower = right % 256
    upper = right // 256
    return (left * lower % modulus + left * upper % modulus * 256) % modulus

def window_taper(pixels):
    places = jnp.arange(pixels, dtype=jnp.float32)
    curve = jnp.sin(math.pi * (places + 0.5) / pixels)
    return 0.25 + 0.75 * curve * curve

def turn_pair(phase_index, modulus):
    angle = phase_index.astype(jnp.float32) * (-two_pi / modulus)
    return (jnp.cos(angle), jnp.sin(angle))

def column_table(facet_ids, pixels, width, modulus, ratio):
    spacing = modulus // pixels
    column_pos = facet_ids // ratio % ratio * pixels
    freqs = spacing * jnp.arange(width, dtype=jnp.int32)
    places = (column_pos[:, None] + jnp.arange(pixels, dtype=jnp.int32)[None, :]) % modulus
    cosine, sine = turn_pair(modmul(freqs[None, :, None], places[:, None, :], modulus), modulus)
    scaled = window_taper(pixels) / math.sqrt(pixels)
    return (jnp.stack([cosine, sine], axis=1) * scaled).astype(jnp.bfloat16)

def row_table(offsets, pixels, width, modulus):
    spacing = modulus // pixels
    freqs = (offsets[:, None] + spacing * jnp.arange(width, dtype=jnp.int32)[None, :]) % modulus
    places = jnp.arange(pixels, dtype=jnp.int32)
    cosine, sine = turn_pair(modmul(freqs[:, :, None], places[None, None, :], modulus), modulus)
    scaled = window_taper(pixels) / math.sqrt(pixels)
    return ((jnp.stack([cosine, sine], axis=1) * scaled).astype(jnp.bfloat16), freqs)

def facet_turn(freqs, facet_ids, modulus, pixels, ratio):
    row_pos = facet_ids % ratio * pixels
    return turn_pair(modmul(freqs[:, :, None], row_pos[None, None, :], modulus), modulus)

def grid_table(size):
    places = jnp.arange(size, dtype=jnp.int32)
    angle = (places[:, None] * places[None, :] % size).astype(jnp.float32) * (two_pi / size)
    return (jnp.stack([jnp.cos(angle), jnp.sin(angle)]) / math.sqrt(size)).astype(jnp.bfloat16)

def slot_table(count, ratio):
    facet_ids = jnp.arange(count, dtype=jnp.int32)
    first = facet_ids % ratio
    second = facet_ids // ratio % ratio
    options = jnp.arange(ratio, dtype=jnp.int32)
    hits = (first[:, None, None] == options[None, :, None]) & (second[:, None, None] == options[None, None, :])
    return hits.astype(jnp.bfloat16)

def as_float(value):
    return value.astype(jnp.float32)

def finish_contrib(raw, turn_real, turn_imag):
    part_real = raw[:, 0, :, :, :, 0] - raw[:, 1, :, :, :, 1]
    part_imag = raw[:, 0, :, :, :, 1] + raw[:, 1, :, :, :, 0]
    real_turn = turn_real[:, :, :, None, None]
    imag_turn = turn_imag[:, :, :, None, None]
    out_real = real_turn * part_real - imag_turn * part_imag
    out_imag = real_turn * part_imag + imag_turn * part_real
    joined = jnp.stack([out_real, out_imag], axis=4)
    return jnp.transpose(joined, (0, 2, 3, 1, 4, 5)).astype(jnp.bfloat16)

def assemble(contrib, slots, grid):
    width = contrib.shape[2]
    terms = contrib.shape[1]
    ratio = slots.shape[1]
    size = width * ratio
    placed = jnp.einsum('fab,ftkcl->katclb', as_float(slots), as_float(contrib))
    amatrix = placed.reshape(size, terms, 2, size).astype(jnp.bfloat16)
    first = jnp.einsum('zum,mtcn->zutcn', as_float(grid), as_float(amatrix))
    front = jnp.stack([first[0, :, :, 0] - first[1, :, :, 1], first[0, :, :, 1] + first[1, :, :, 0]], axis=2).astype(jnp.bfloat16)
    second = jnp.einsum('utcn,zvn->utczv', as_float(front), as_float(grid))
    sky_real = second[:, :, 0, 0] - second[:, :, 1, 1]
    sky_imag = second[:, :, 0, 1] + second[:, :, 1, 0]
    return jnp.stack([sky_real, sky_imag], axis=2).astype(jnp.bfloat16)

def degrid_grid(sky_grid, rows, count, observed):
    slots_count, channels, tile_height, span = observed.shape
    size = sky_grid.shape[0]
    nu_values = (jnp.arange(channels, dtype=jnp.float32) + 0.5) / channels - 0.5
    live = jnp.arange(slots_count, dtype=jnp.int32) < count
    target = rows[:, None] + jnp.arange(tile_height, dtype=jnp.int32)[None, :]
    hits = (target[:, :, None] == jnp.arange(size, dtype=jnp.int32)[None, None, :]) & live[:, None, None]
    placer = hits.astype(jnp.bfloat16).reshape(slots_count * tile_height, size)
    model_rows = jnp.dot(placer, sky_grid.reshape(size, 2 * span), preferred_element_type=jnp.float32)
    model_rows = model_rows.reshape(slots_count, tile_height, 2, span)
    model = model_rows[:, None, :, 0] + nu_values[None, :, None, None] * model_rows[:, None, :, 1]
    residual = (observed.astype(jnp.float32) - model) * live[:, None, None, None].astype(jnp.float32)
    weighted = jnp.stack([lax.optimization_barrier(jnp.sum(residual, axis=1)), lax.optimization_barrier(jnp.sum(nu_values[None, :, None, None] * residual, axis=1))], axis=2)
    weighted = weighted.astype(jnp.bfloat16).reshape(slots_count * tile_height, 2 * span)
    regrid = lax.dot_general(placer, weighted, (((0,), (0,)), ((), ())), preferred_element_type=jnp.float32)
    return (residual.astype(jnp.bfloat16), regrid.reshape(size, 2, 2, size).astype(jnp.bfloat16))

def adjoint_grid(regrid, grid):
    first = jnp.einsum('zum,utcv->zmtcv', as_float(grid), as_float(regrid))
    back_real = first[0, :, :, 0] + first[1, :, :, 1]
    back_imag = first[0, :, :, 1] - first[1, :, :, 0]
    back_front = jnp.stack([back_real, back_imag], axis=2).astype(jnp.bfloat16)
    second = jnp.einsum('mtcv,zvn->mtczn', as_float(back_front), as_float(grid))
    grid_real = second[:, :, 0, 0] + second[:, :, 1, 1]
    grid_imag = second[:, :, 1, 0] - second[:, :, 0, 1]
    return jnp.stack([grid_real, grid_imag], axis=2).astype(jnp.bfloat16)

def select_slots(back_grid, slots):
    ratio = slots.shape[1]
    size = back_grid.shape[0]
    width = size // ratio
    terms = back_grid.shape[1]
    shaped = back_grid.reshape(width, ratio, terms, 2, width, ratio)
    return jnp.einsum('fab,katclb->ftkcl', as_float(slots), as_float(shaped)).astype(jnp.bfloat16)

def turn_back(returned, turn_real, turn_imag):
    real_turn = jnp.transpose(turn_real, (0, 2, 1))[:, :, None, :, None]
    imag_turn = jnp.transpose(turn_imag, (0, 2, 1))[:, :, None, :, None]
    part_real = returned[:, :, :, :, 0].astype(jnp.float32)
    part_imag = returned[:, :, :, :, 1].astype(jnp.float32)
    turned = jnp.stack([real_turn * part_real + imag_turn * part_imag, real_turn * part_imag - imag_turn * part_real], axis=4)
    return turned.astype(jnp.bfloat16)

def paired_terms(turned):
    real_part = turned[:, :, :, :, 0]
    imag_part = turned[:, :, :, :, 1]
    pair_real = jnp.stack([real_part, imag_part], axis=1)
    pair_imag = jnp.stack([imag_part, -real_part], axis=1)
    return jnp.stack([pair_real, pair_imag], axis=5)

def strip_terms(table_part, turned):
    return jnp.einsum('szkp,szftkcl->pftcl', as_float(table_part), as_float(paired_terms(turned)))

def reference(facet_model, sub_offsets, tile_rows, tile_counts, visibilities):
    ratio = SG // CS
    facet_ids = jnp.arange(NF, dtype=jnp.int32)
    columns = column_table(facet_ids, FP, CS, SKY, ratio)
    strips = jnp.einsum('tfpq,fckq->pftck', as_float(facet_model), as_float(columns)).astype(jnp.bfloat16)
    slots = slot_table(NF, ratio)
    grid = grid_table(SG)

    def one_subgrid(carry, inputs):
        offset, rows, count, observed = inputs
        rtable, freqs = row_table(offset[None], FP, CS, SKY)
        turn_real, turn_imag = facet_turn(freqs, facet_ids, SKY, FP, ratio)
        raw = jnp.einsum('szkp,pftcl->szkftcl', as_float(rtable), as_float(strips))
        contrib = finish_contrib(raw, turn_real, turn_imag)[0]
        sky_grid = assemble(contrib, slots, grid)
        residual, regrid = degrid_grid(sky_grid, rows, count, observed)
        back_grid = adjoint_grid(regrid, grid)
        returned = select_slots(back_grid, slots)[None]
        turned = turn_back(returned, turn_real, turn_imag)
        return (carry + strip_terms(rtable, turned), residual)
    start = jnp.zeros((FP, NF, 2, 2, CS), jnp.float32)
    strip_sum, residual_vis = lax.scan(one_subgrid, start, (sub_offsets, tile_rows, tile_counts, visibilities))
    strip_round = strip_sum.astype(jnp.bfloat16)
    residual_facets = jnp.einsum('pftck,fckq->tfpq', as_float(strip_round), as_float(columns)).astype(jnp.bfloat16)
    return (residual_facets, residual_vis)
```

```python
import math

import jax
import jax.numpy as jnp
from jax import lax
from jax.experimental import pallas as pl
from jax.experimental.pallas import tpu as pltpu
from jax.sharding import Mesh
from jax.sharding import PartitionSpec as P

SKY = 65536
FP = 8192
CS = 64
SG = 128
TM = 4
TR = 8
CH = 32
W = TM * TR
PB = 64
ROWS = 8
LP = ROWS * PB
LS = 32
QT = 1024

f32 = jnp.float32
bf16 = jnp.bfloat16


def turn(index, period):
    quarter = period // 4
    quadrant = (index + quarter // 2) // quarter
    x = (index - quadrant * quarter).astype(f32) * (2.0 * math.pi / period)
    y = x * x
    sine = x * (1.0 + y * (-1.0 / 6 + y * (1.0 / 120 + y * (-1.0 / 5040 + y * (1.0 / 362880)))))
    cosine = 1.0 + y * (-0.5 + y * (1.0 / 24 + y * (-1.0 / 720 + y * (1.0 / 40320 - y * (1.0 / 3628800)))))
    swap = (quadrant & 1) == 1
    first = jnp.where(swap, sine, cosine)
    second = jnp.where(swap, cosine, sine)
    first = jnp.where((quadrant == 1) | (quadrant == 2), -first, first)
    second = jnp.where((quadrant & 3) >= 2, -second, second)
    return first, second


def taper(place):
    cosine, _ = turn(2 * place + 1, 2 * FP)
    return 0.625 - 0.375 * cosine


def iota(shape, dim):
    return lax.broadcasted_iota(jnp.int32, shape, dim)


def strips_kernel(model_ref, out_ref, table_ref, acc_ref):
    step = pl.program_id(0)
    place = step * QT + iota((8, QT), 1)
    line = iota((8, QT), 0)
    scale = taper(place) * (1.0 / math.sqrt(FP))
    low_re, low_im = turn((line * place) & (FP - 1), FP)
    low_re, low_im = low_re * scale, low_im * scale
    high_re, high_im = turn((8 * line * place) & (FP - 1), FP)
    real, imag = [], []
    for k in range(8):
        re, im = high_re[k : k + 1], high_im[k : k + 1]
        real.append(low_re * re - low_im * im)
        imag.append(-(low_re * im + low_im * re))
    table = jnp.concatenate(real + imag, axis=0).astype(bf16)
    table_ref[...] = table
    model = model_ref[...].reshape(4 * PB, QT)
    part = lax.dot_general(model, table, (((1,), (1,)), ((), ())), preferred_element_type=f32)

    @pl.when(step == 0)
    def _():
        acc_ref[...] = part

    @pl.when(step > 0)
    def _():
        acc_ref[...] += part

    @pl.when(step == FP // QT - 1)
    def _():
        parts = []
        for a in range(2):
            for t in range(2):
                at = (t * 2 + a) * PB
                parts.append(acc_ref[at : at + PB, :])
        strip = jnp.concatenate(parts, axis=1).astype(bf16)
        for r in range(ROWS):
            out_ref[r] = strip


def strips_call(model):
    return pl.pallas_call(
        strips_kernel,
        grid=(FP // QT,),
        in_specs=[pl.BlockSpec((2, 2, PB, QT), lambda i: (0, 0, 0, i))],
        out_specs=[
            pl.BlockSpec((ROWS, PB, 8 * CS), lambda i: (0, 0, 0)),
            pl.BlockSpec((2 * CS, QT), lambda i: (0, i)),
        ],
        out_shape=[
            jax.ShapeDtypeStruct((ROWS, PB, 8 * CS), bf16),
            jax.ShapeDtypeStruct((2 * CS, FP), bf16),
        ],
        scratch_shapes=[pltpu.VMEM((4 * PB, 2 * CS), f32)],
        cost_estimate=pl.CostEstimate(flops=2 * 256 * 128 * FP, bytes_accessed=7 << 20, transcendentals=0),
        name="strips",
    )(model)


def operator_kernel(offsets_ref, tiles_ref, where_ref, h_ref, tre_ref, tim_ref, d_ref, e_ref):
    step = pl.program_id(0)
    core, row, base = where_ref[0], where_ref[1], where_ref[2]

    @pl.when(step == 0)
    def _():
        u = iota((SG, LP), 0)
        p = base + iota((SG, LP), 1)
        n = (SG * u - p) & (FP - 1)
        _, under = turn(n, 2 * FP)
        _, over = turn((CS * n) & (2 * FP - 1), 2 * FP)
        ratio = jnp.where(n == 0, float(CS), over / jnp.where(n == 0, 1.0, under))
        ratio = ratio * taper(p) * (1.0 / 1024)
        re, im = turn(((CS - 1) * n) & (2 * FP - 1), 2 * FP)
        re, im = re * ratio, im * ratio
        cu, su = turn(u, SG)
        for i, part in enumerate((re, im, re * cu - im * su, re * su + im * cu)):
            for q in range(LP // 128):
                d_ref[i, q] = part[:, q * 128 : (q + 1) * 128]

    lane = iota((8, LP), 1) + base
    line = iota((8, LP), 0)
    offset = jnp.zeros((8, LP), jnp.int32)
    index = []
    for i in range(4):
        g = step * 4 + i
        o, z, b = g // 16, (g // 2) % 8, g % 2
        c = core + o - 2 * core * o
        facet = z * 2 + c
        index.append(facet * 2 + b)
        off = offsets_ref[2 * (facet * ROWS + row) + b]
        offset = jnp.where((line & 3) == i, off, offset)
    place = lane + jnp.where(line >= 4, FP, 0)
    cosine, sine = turn((offset * place) & (SKY - 1), SKY)
    e_ref[0] = cosine
    e_ref[1] = -sine
    blocks = [[] for _ in range(4)]
    for i in range(4):
        for j in range(TM):
            at = tiles_ref[index[i] * TM + j]
            for a in range(2):
                er = e_ref[0, a * 4 + i : a * 4 + i + 1, :]
                ei = e_ref[1, a * 4 + i : a * 4 + i + 1, :]
                dr = jnp.concatenate([d_ref[2 * a, q, pl.ds(at, TR), :] for q in range(LP // 128)], axis=1)
                di = jnp.concatenate([d_ref[2 * a + 1, q, pl.ds(at, TR), :] for q in range(LP // 128)], axis=1)
                blocks[2 * a].append(dr * er - di * ei)
                blocks[2 * a + 1].append(dr * ei + di * er)
    for a in range(2):
        for c in range(2):
            block = jnp.concatenate(blocks[2 * a + c], axis=0)
            h_ref[:, (2 * a + c) * LP : (2 * a + c + 1) * LP] = block.astype(bf16)
            out = tre_ref if c == 0 else tim_ref
            out[a * LP : (a + 1) * LP, :] = block.T.astype(bf16)


def operator_call(offsets, tiles, where):
    smem = pl.BlockSpec(memory_space=pltpu.SMEM)
    return pl.pallas_call(
        operator_kernel,
        grid=(LS // 4,),
        in_specs=[smem, smem, smem],
        out_specs=[
            pl.BlockSpec((4 * W, 4 * LP), lambda i: (i, 0)),
            pl.BlockSpec((2 * LP, 4 * W), lambda i: (0, i)),
            pl.BlockSpec((2 * LP, 4 * W), lambda i: (0, i)),
        ],
        out_shape=[
            jax.ShapeDtypeStruct((LS * W, 4 * LP), bf16),
            jax.ShapeDtypeStruct((2 * LP, LS * W), bf16),
            jax.ShapeDtypeStruct((2 * LP, LS * W), bf16),
        ],
        scratch_shapes=[pltpu.VMEM((4, LP // 128, SG, 128), f32), pltpu.VMEM((2, 8, LP), f32)],
        cost_estimate=pl.CostEstimate(flops=20 << 20, bytes_accessed=8 << 20, transcendentals=0),
        name="operator",
    )(offsets, tiles, where)


def cross(x, sign):
    rows, lanes = x.shape
    left = iota((rows, 2 * CS), 1) < CS
    parts = []
    for at in range(0, lanes, 2 * CS):
        turned = pltpu.roll(x[:, at : at + 2 * CS].astype(f32), CS, 1)
        parts.append(jnp.where(left, -sign * turned, sign * turned).astype(bf16))
    return jnp.concatenate(parts, axis=1)


def fore_kernel(h_ref, strips_ref, own_ref, other_ref, rhs_ref):
    step = pl.program_id(0)

    @pl.when(step == 0)
    def _():
        strips = strips_ref[...].reshape(LP, 8 * CS)
        crossed = cross(strips, 1.0)
        for a in range(2):
            rhs_ref[2 * a * LP : (2 * a + 1) * LP, :] = strips[:, a * 4 * CS : (a + 1) * 4 * CS]
            rhs_ref[(2 * a + 1) * LP : (2 * a + 2) * LP, :] = crossed[:, a * 4 * CS : (a + 1) * 4 * CS]

    out = jnp.dot(h_ref[...], rhs_ref[...], preferred_element_type=f32)
    out = out.reshape(8, W, 4 * CS).astype(bf16)

    @pl.when(step < 2)
    def _():
        own_ref[...] = out

    @pl.when(step >= 2)
    def _():
        other_ref[...] = out


def fore_call(h, strips):
    return pl.pallas_call(
        fore_kernel,
        grid=(4,),
        in_specs=[
            pl.BlockSpec((8 * W, 4 * LP), lambda i: (i, 0)),
            pl.BlockSpec((ROWS, PB, 8 * CS), lambda i: (0, 0, 0)),
        ],
        out_specs=[
            pl.BlockSpec((8, W, 4 * CS), lambda i: (jnp.minimum(i, 1), 0, 0)),
            pl.BlockSpec((8, W, 4 * CS), lambda i: (jnp.maximum(i, 2) - 2, 0, 0)),
        ],
        out_shape=[jax.ShapeDtypeStruct((LS // 2, W, 4 * CS), bf16)] * 2,
        scratch_shapes=[pltpu.VMEM((4 * LP, 4 * CS), bf16)],
        cost_estimate=pl.CostEstimate(flops=2 << 30, bytes_accessed=5 << 20, transcendentals=0),
        name="fore",
    )(h, strips)


def subgrid_kernel(count_ref, parts_ref, vis_ref, res_ref, out_ref):
    l = iota((2 * CS, SG), 0) & (CS - 1)
    upper = iota((2 * CS, SG), 0) < CS
    v = iota((2 * CS, SG), 1)
    rows = []
    for b in range(2):
        cosine, sine = turn((v * (2 * l + b)) & (SG - 1), SG)
        real = jnp.where(upper, cosine, -sine)
        imag = jnp.where(upper, sine, cosine)
        rows.append(jnp.concatenate([real, imag], axis=1))
    table = (jnp.concatenate(rows, axis=0) * (1.0 / math.sqrt(SG))).astype(bf16)

    fronts = []
    for b in range(2):
        total = parts_ref[b].astype(f32)
        for z in range(1, 8):
            total = total + parts_ref[2 * z + b].astype(f32)
        fronts.append(total.astype(bf16))
    front = jnp.concatenate(
        [jnp.concatenate([fronts[b][:, t * 2 * CS : (t + 1) * 2 * CS] for b in range(2)], axis=1) for t in range(2)],
        axis=0,
    )
    sky = jnp.dot(front, table, preferred_element_type=f32).astype(bf16).astype(f32)
    count = count_ref[0]
    weighted = [[], []]
    for j in range(TM):
        m0 = sky[j * TR : (j + 1) * TR]
        m1 = sky[W + j * TR : W + (j + 1) * TR]
        live = jnp.where(j < count, 1.0, 0.0)
        w0 = jnp.zeros((TR, 2 * SG), f32)
        w1 = jnp.zeros((TR, 2 * SG), f32)
        for c in range(CH):
            nu = (c + 0.5) / CH - 0.5
            res = (vis_ref[j, c].astype(f32) - (m0 + nu * m1)) * live
            res_ref[j, c] = res.astype(bf16)
            w0 = w0 + res
            w1 = w1 + nu * res
        weighted[0].append(w0)
        weighted[1].append(w1)
    weight = jnp.concatenate(weighted[0] + weighted[1], axis=0).astype(bf16)
    back = lax.dot_general(weight, table, (((1,), (1,)), ((), ())), preferred_element_type=f32).astype(bf16)
    for b in range(2):
        block = jnp.concatenate([back[t * W : (t + 1) * W, b * 2 * CS : (b + 1) * 2 * CS] for t in range(2)], axis=1)
        for z in range(8):
            out_ref[2 * z + b] = block


def subgrid_call(count, parts, vis):
    return pl.pallas_call(
        subgrid_kernel,
        in_specs=[
            pl.BlockSpec(memory_space=pltpu.SMEM),
            pl.BlockSpec(memory_space=pltpu.VMEM),
            pl.BlockSpec(memory_space=pltpu.VMEM),
        ],
        out_specs=[pl.BlockSpec(memory_space=pltpu.VMEM)] * 2,
        out_shape=[
            jax.ShapeDtypeStruct((TM, CH, TR, 2 * SG), bf16),
            jax.ShapeDtypeStruct((LS // 2, W, 4 * CS), bf16),
        ],
        cost_estimate=pl.CostEstimate(flops=20 << 20, bytes_accessed=2 << 20, transcendentals=0),
        name="subgrid",
    )(count, parts, vis)


def back_kernel(tre_ref, tim_ref, own_ref, other_ref, out_ref, rhs_ref):
    step = pl.program_id(0)
    half = LS * W // 2

    @pl.when(step == 0)
    def _():
        for o, ref in enumerate((own_ref, other_ref)):
            rows = ref[...].reshape(half, 4 * CS)
            rhs_ref[o * half : (o + 1) * half, :] = rows
            rhs_ref[(2 + o) * half : (3 + o) * half, :] = cross(rows, -1.0)

    out = jnp.dot(tre_ref[...], rhs_ref[: 2 * half], preferred_element_type=f32)
    out = out + jnp.dot(tim_ref[...], rhs_ref[2 * half :], preferred_element_type=f32)
    out_ref[...] = out.reshape(4, PB, 4 * CS).astype(bf16)


def back_call(tre, tim, own, other):
    whole = pl.BlockSpec((LS // 2, W, 4 * CS), lambda i: (0, 0, 0))
    return pl.pallas_call(
        back_kernel,
        grid=(4,),
        in_specs=[
            pl.BlockSpec((4 * PB, LS * W), lambda i: (i, 0)),
            pl.BlockSpec((4 * PB, LS * W), lambda i: (i, 0)),
            whole,
            whole,
        ],
        out_specs=pl.BlockSpec((4, PB, 4 * CS), lambda i: (i % 2, 0, i // 2)),
        out_shape=jax.ShapeDtypeStruct((ROWS, PB, 8 * CS), bf16),
        scratch_shapes=[pltpu.VMEM((2 * LS * W, 4 * CS), bf16)],
        cost_estimate=pl.CostEstimate(flops=2 << 30, bytes_accessed=6 << 20, transcendentals=0),
        name="back",
    )(tre, tim, own, other)


def facets_kernel(parts_ref, table_ref, out_ref, lhs_ref):
    @pl.when(pl.program_id(0) == 0)
    def _():
        total = parts_ref[0].astype(f32)
        for r in range(1, ROWS):
            total = total + parts_ref[r].astype(f32)
        total = total.astype(bf16)
        for a in range(2):
            for t in range(2):
                at = (a * 2 + t) * 2 * CS
                lhs_ref[(t * 2 + a) * PB : (t * 2 + a + 1) * PB, :] = total[:, at : at + 2 * CS]

    out = jnp.dot(lhs_ref[...], table_ref[...], preferred_element_type=f32)
    out_ref[...] = out.reshape(2, 2, PB, QT).astype(bf16)


def facets_call(parts, table):
    return pl.pallas_call(
        facets_kernel,
        grid=(FP // QT,),
        in_specs=[
            pl.BlockSpec((ROWS, PB, 8 * CS), lambda i: (0, 0, 0)),
            pl.BlockSpec((2 * CS, QT), lambda i: (0, i)),
        ],
        out_specs=pl.BlockSpec((2, 2, PB, QT), lambda i: (0, 0, 0, i)),
        out_shape=jax.ShapeDtypeStruct((2, 2, PB, FP), bf16),
        scratch_shapes=[pltpu.VMEM((4 * PB, 2 * CS), bf16)],
        cost_estimate=pl.CostEstimate(flops=2 * 256 * 128 * FP, bytes_accessed=7 << 20, transcendentals=0),
        name="facets",
    )(parts, table)


def local(facet_model, sub_offsets, tile_rows, tile_counts, visibilities):
    core = lax.axis_index("core")
    row = lax.axis_index("row")
    facet = lax.axis_index("z") * 2 + core
    where = jnp.stack([core, row, facet * LP]).astype(jnp.int32)

    tiles = lax.all_to_all(
        jnp.broadcast_to(tile_rows, (LS, TM)), ("z", "core", "sub"), split_axis=0, concat_axis=0, tiled=True
    ).reshape(LS * TM)
    strips, table = strips_call(facet_model)
    strips = lax.all_to_all(strips, "row", split_axis=0, concat_axis=0, tiled=True)
    h, tre, tim = operator_call(sub_offsets, tiles, where)

    swap = [(0, 1), (1, 0)]
    own, other = fore_call(h, strips)
    other = lax.ppermute(other, "core", swap)
    parts = (own.astype(f32) + other.astype(f32)).astype(bf16)
    parts = lax.all_to_all(parts, ("z", "sub"), split_axis=0, concat_axis=0, tiled=True)
    residual, back = subgrid_call(tile_counts, parts, visibilities[0])
    own = lax.all_to_all(back, ("z", "sub"), split_axis=0, concat_axis=0, tiled=True)
    other = lax.ppermute(own, "core", swap)
    sums = back_call(tre, tim, own, other)
    sums = lax.all_to_all(sums, "row", split_axis=0, concat_axis=0, tiled=True)
    return facets_call(sums, table), residual[None]


def solution(mesh):
    split = Mesh(mesh.devices.reshape(8, 2, 8, 2), ("z", "core", "row", "sub"))
    whole = ("z", "core", "row", "sub")
    model = P(None, "sub", ("z", "core", "row"), None)
    return jax.shard_map(
        local,
        mesh=split,
        in_specs=(model, P(), P(whole, None), P(whole), P(whole, None, None, None, None)),
        out_specs=(model, P(whole, None, None, None, None)),
        check_vma=False,
    )
```

```python
import math

import jax
import jax.numpy as jnp
from jax import lax
from jax.experimental import pallas as pl
from jax.experimental.pallas import tpu as pltpu
from jax.sharding import Mesh
from jax.sharding import PartitionSpec as P

SKY = 65536
FP = 8192
CS = 64
SG = 128
TM = 4
TR = 8
CH = 32
W = TM * TR
PB = 64
ROWS = 8
LP = ROWS * PB
LS = 32
QT = 1024

f32 = jnp.float32
bf16 = jnp.bfloat16


def turn(index, period):
    quarter = period // 4
    quadrant = lax.shift_right_logical(index + quarter // 2, quarter.bit_length() - 1)
    x = (index - quadrant * quarter).astype(f32) * (2.0 * math.pi / period)
    y = x * x
    sine = x * (1.0 + y * (-1.0 / 6 + y * (1.0 / 120 + y * (-1.0 / 5040 + y * (1.0 / 362880)))))
    cosine = 1.0 + y * (-0.5 + y * (1.0 / 24 + y * (-1.0 / 720 + y * (1.0 / 40320 - y * (1.0 / 3628800)))))
    swap = (quadrant & 1) == 1
    first = jnp.where(swap, sine, cosine)
    second = jnp.where(swap, cosine, sine)
    first = jnp.where(((quadrant + 1) & 2) == 2, -first, first)
    second = jnp.where((quadrant & 2) == 2, -second, second)
    return first, second


def taper(place):
    cosine, _ = turn(2 * place + 1, 2 * FP)
    return 0.625 - 0.375 * cosine


def iota(shape, dim):
    return lax.broadcasted_iota(jnp.int32, shape, dim)


def column_start(base_ref):
    place = iota((8, QT), 1)
    line = iota((8, QT), 0)
    tables = turn((line * place) & (QT - 1), QT) + turn((line * place) & (FP - 1), FP) + turn(2 * place + 1, 2 * FP)
    for i, table in enumerate(tables):
        base_ref[i] = table


def column_block(base_ref, step):
    wide = lambda x: jnp.concatenate([x] * (QT // 128), axis=1)
    move_re, move_im = (wide(x) for x in turn((iota((8, 128), 0) * step) & 7, 8))
    tilt_re, tilt_im = (wide(x) for x in turn(jnp.full((8, 128), step, jnp.int32), 8))
    cosine = base_ref[4] * tilt_re - base_ref[5] * tilt_im
    scale = (0.625 - 0.375 * cosine) * (1.0 / math.sqrt(FP))
    low_re = (base_ref[2] * move_re - base_ref[3] * move_im) * scale
    low_im = (base_ref[2] * move_im + base_ref[3] * move_re) * scale
    real, imag = [], []
    for k in range(8):
        re, im = base_ref[0, k : k + 1], base_ref[1, k : k + 1]
        real.append(low_re * re - low_im * im)
        imag.append(-(low_re * im + low_im * re))
    return jnp.concatenate(real + imag, axis=0).astype(bf16)


def subgrid_of(g):
    core = lax.axis_index("core")
    o, z, b = g // 16, (g // 2) % 8, g % 2
    c = core + o - 2 * core * o
    facet = z * 2 + c
    return facet * 2 + b, 2 * (facet * 8 + lax.axis_index("xh") * 4 + lax.axis_index("y")) + b


def line_rows(shape):
    z = lax.axis_index("zh") * 2 + lax.axis_index("zl")
    return (z * 2 + lax.axis_index("core")) * LP + iota(shape, 1)


def phase_table(ref):
    shape = (SG + TR, 2 * CS)
    cosine, sine = turn(iota(shape, 0) & (SG - 1), SG)
    ref[0] = cosine
    ref[1] = jnp.where(iota(shape, 1) < CS, -sine, sine)


def phases(ref, tiles_ref, offsets_ref, first):
    parts = [[], []]
    for i in range(8):
        index, s = subgrid_of(first + i)
        for j in range(TM):
            at = (tiles_ref[index, j] - 16 * offsets_ref[s]) & (SG - 1)
            for c in range(2):
                parts[c].append(ref[c, pl.ds(at, TR), :])
    real, imag = (jnp.concatenate(x, axis=0) for x in parts)
    return jnp.concatenate([real, real], axis=1), jnp.concatenate([imag, imag], axis=1)


def swapped(x):
    return jnp.concatenate([pltpu.roll(x[:, i : i + 2 * CS], CS, 1) for i in range(0, x.shape[1], 2 * CS)], axis=1)


SMEM = pl.BlockSpec(memory_space=pltpu.SMEM)
VMEM = pl.BlockSpec(memory_space=pltpu.VMEM)
HBM = pl.BlockSpec(memory_space=pltpu.HBM)


def params(mib):
    return pltpu.CompilerParams(vmem_limit_bytes=mib << 20)


def strips_kernel(model_ref, out_ref, buffer, sems, base_ref, table_ref):
    rows = PB // 2

    def copy(i):
        return pltpu.make_async_copy(
            model_ref.at[i // 4, (i // 2) % 2, pl.ds((i % 2) * rows, rows), :], buffer.at[i], sems.at[i]
        )

    for i in range(8):
        copy(i).start()
    column_start(base_ref)

    def body(i, carry):
        table_ref[:, pl.ds(pl.multiple_of(i * QT, QT), QT)] = column_block(base_ref, i)
        return carry

    lax.fori_loop(0, FP // QT, body, 0)
    for i in range(8):
        copy(i).wait()
    strips = lax.dot_general(
        buffer[...].reshape(4 * PB, FP), table_ref[...], (((1,), (1,)), ((), ())), preferred_element_type=f32
    ).astype(bf16)
    parts = [strips[(t * 2 + a) * PB : (t * 2 + a + 1) * PB] for a in range(2) for t in range(2)]
    strip = jnp.concatenate(parts, axis=1)
    for r in range(ROWS):
        out_ref[r] = strip


def strips_call(model):
    return pl.pallas_call(
        strips_kernel,
        in_specs=[HBM],
        out_specs=VMEM,
        out_shape=jax.ShapeDtypeStruct((ROWS, PB, 8 * CS), bf16),
        scratch_shapes=[
            pltpu.VMEM((8, PB // 2, FP), bf16),
            pltpu.SemaphoreType.DMA((8,)),
            pltpu.VMEM((6, 8, QT), f32),
            pltpu.VMEM((2 * CS, FP), bf16),
        ],
        compiler_params=params(60),
        cost_estimate=pl.CostEstimate(flops=2 * 256 * 128 * FP, bytes_accessed=5 << 20, transcendentals=0),
        name="strips",
    )(model)


def waves_kernel(d_ref):
    p = line_rows((TR, LP))
    line = iota((TR, LP), 0)

    def body(i, carry):
        n = (SG * (i * TR + line) - p) & (FP - 1)
        _, under = turn(n, 2 * FP)
        _, over = turn((CS * n) & (2 * FP - 1), 2 * FP)
        ratio = jnp.where(n == 0, float(CS), over / jnp.where(n == 0, 1.0, under))
        re, im = turn(((CS - 1) * n) & (2 * FP - 1), 2 * FP)
        for c, part in enumerate((re * ratio, im * ratio)):
            for q in range(LP // 128):
                d_ref[c, q, pl.ds(pl.multiple_of(i * TR, TR), TR), :] = part[:, q * 128 : (q + 1) * 128]
        return carry

    lax.fori_loop(0, SG // TR, body, 0)


def waves_call():
    return pl.pallas_call(
        waves_kernel,
        out_specs=VMEM,
        out_shape=jax.ShapeDtypeStruct((2, LP // 128, SG, 128), f32),
        compiler_params=params(24),
        cost_estimate=pl.CostEstimate(flops=8 << 20, bytes_accessed=1 << 20, transcendentals=0),
        name="waves",
    )()


def operator_kernel(tiles_ref, offsets_ref, count_ref, d_ref, h_ref, live_ref, e_ref):
    live_ref[...] = jnp.where(iota((W, 128), 0) < TR * count_ref[0], 1.0, 0.0)
    place = line_rows((8, LP))
    line = iota((8, LP), 0)
    scale = taper(place) * (1.0 / 1024)

    def body(step, carry):
        offset = jnp.zeros((8, LP), jnp.int32)
        index = []
        for i in range(8):
            at, s = subgrid_of(step * 8 + i)
            index.append(at)
            offset = jnp.where(line == i, offsets_ref[s], offset)
        cosine, sine = turn((offset * place) & (SKY - 1), SKY)
        e_ref[0] = cosine * scale
        e_ref[1] = -sine * scale
        for half in range(2):
            real, imag = [], []
            for i in range(4 * half, 4 * half + 4):
                er = e_ref[0, i : i + 1, :]
                ei = e_ref[1, i : i + 1, :]
                for j in range(TM):
                    at = tiles_ref[index[i], j]
                    dr = jnp.concatenate([d_ref[0, q, pl.ds(at, TR), :] for q in range(LP // 128)], axis=1)
                    di = jnp.concatenate([d_ref[1, q, pl.ds(at, TR), :] for q in range(LP // 128)], axis=1)
                    real.append(dr * er - di * ei)
                    imag.append(dr * ei + di * er)
            rows = pl.ds(pl.multiple_of(step * 8 * W + half * 4 * W, 4 * W), 4 * W)
            h_ref[rows, :LP] = jnp.concatenate(real, axis=0).astype(bf16)
            h_ref[rows, LP:] = jnp.concatenate(imag, axis=0).astype(bf16)
        return carry

    lax.fori_loop(0, LS // 8, body, 0)


def operator_call(tiles, offsets, count, waves):
    return pl.pallas_call(
        operator_kernel,
        in_specs=[SMEM, SMEM, SMEM, VMEM],
        out_specs=[VMEM, VMEM],
        out_shape=[jax.ShapeDtypeStruct((LS * W, 2 * LP), bf16), jax.ShapeDtypeStruct((W, 128), f32)],
        scratch_shapes=[pltpu.VMEM((2, 8, LP), f32)],
        compiler_params=params(24),
        cost_estimate=pl.CostEstimate(flops=20 << 20, bytes_accessed=8 << 20, transcendentals=0),
        name="operator",
    )(tiles, offsets, count, waves)


def fore_kernel(tiles_ref, offsets_ref, h_ref, strips_ref, own_ref, other_ref, rhs_ref, phase_ref):
    phase_table(phase_ref)
    left = iota((PB, 2 * CS), 1) < CS
    for r in range(ROWS):
        strips = strips_ref[r]
        rhs_ref[r * PB : (r + 1) * PB, :] = strips
        for at in range(0, 8 * CS, 2 * CS):
            turned = pltpu.roll(strips[:, at : at + 2 * CS].astype(f32), CS, 1)
            rhs_ref[LP + r * PB : LP + (r + 1) * PB, at : at + 2 * CS] = jnp.where(left, -turned, turned).astype(bf16)
    rows = 8 * W
    for step in range(4):
        out = jnp.dot(h_ref[step * rows : (step + 1) * rows, :], rhs_ref[...], preferred_element_type=f32)
        real, imag = phases(phase_ref, tiles_ref, offsets_ref, step * 8)
        second = out[:, 4 * CS :]
        out = out[:, : 4 * CS] + second * real + swapped(second) * imag
        ref = own_ref if step < 2 else other_ref
        ref[step % 2 * 8 : step % 2 * 8 + 8] = out.reshape(8, W, 4 * CS).astype(bf16)


def fore_call(tiles, offsets, h, strips):
    return pl.pallas_call(
        fore_kernel,
        in_specs=[SMEM, SMEM, VMEM, VMEM],
        out_specs=[VMEM, VMEM],
        out_shape=[jax.ShapeDtypeStruct((LS // 2, W, 4 * CS), bf16)] * 2,
        scratch_shapes=[
            pltpu.VMEM((2 * LP, 8 * CS), bf16),
            pltpu.VMEM((2, SG + TR, 2 * CS), f32),
        ],
        compiler_params=params(24),
        cost_estimate=pl.CostEstimate(flops=1 << 30, bytes_accessed=4 << 20, transcendentals=0),
        name="fore",
    )(tiles, offsets, h, strips)


def add_kernel(own_ref, other_ref, out_ref):
    out_ref[...] = (own_ref[...].astype(f32) + other_ref[...].astype(f32)).astype(bf16)


def add_call(own, other):
    return pl.pallas_call(
        add_kernel,
        in_specs=[VMEM, VMEM],
        out_specs=VMEM,
        out_shape=jax.ShapeDtypeStruct(own.shape, bf16),
        compiler_params=params(24),
        cost_estimate=pl.CostEstimate(flops=1 << 18, bytes_accessed=1 << 20, transcendentals=0),
        name="add",
    )(own, other)


def subgrid_kernel(live_ref, parts_ref, vis_ref, res_ref, out_ref, buffer, sems):
    l = iota((2 * CS, SG), 0) & (CS - 1)
    upper = iota((2 * CS, SG), 0) < CS
    v = iota((2 * CS, SG), 1)
    rows = []
    for b in range(2):
        cosine, sine = turn((v * (2 * l + b)) & (SG - 1), SG)
        real = jnp.where(upper, cosine, -sine)
        imag = jnp.where(upper, sine, cosine)
        rows.append(jnp.concatenate([real, imag], axis=1))
    table = (jnp.concatenate(rows, axis=0) * (1.0 / math.sqrt(SG))).astype(bf16)

    fronts = []
    for b in range(2):
        total = parts_ref[b].astype(f32)
        for z in range(1, 8):
            total = total + parts_ref[2 * z + b].astype(f32)
        fronts.append(total.astype(bf16))
    front = jnp.concatenate(
        [jnp.concatenate([fronts[b][:, t * 2 * CS : (t + 1) * 2 * CS] for b in range(2)], axis=1) for t in range(2)],
        axis=0,
    )
    sky = jnp.dot(front, table, preferred_element_type=f32).astype(bf16).astype(f32)
    weighted = [[], []]
    for j in range(TM):
        m0 = sky[j * TR : (j + 1) * TR]
        m1 = sky[W + j * TR : W + (j + 1) * TR]
        live = live_ref[j * TR : (j + 1) * TR, :]
        live = jnp.concatenate([live, live], axis=1)
        w0 = jnp.zeros((TR, 2 * SG), f32)
        w1 = jnp.zeros((TR, 2 * SG), f32)
        for c in range(CH):
            nu = (c + 0.5) / CH - 0.5
            res = (vis_ref[j, c].astype(f32) - (m0 + nu * m1)) * live
            buffer[j, c] = res.astype(bf16)
            w0 = w0 + res
            w1 = w1 + nu * res
        pltpu.make_async_copy(buffer.at[j], res_ref.at[j], sems.at[j]).start()
        weighted[0].append(w0)
        weighted[1].append(w1)
    weight = jnp.concatenate(weighted[0] + weighted[1], axis=0).astype(bf16)
    back = lax.dot_general(weight, table, (((1,), (1,)), ((), ())), preferred_element_type=f32).astype(bf16)
    for b in range(2):
        block = jnp.concatenate([back[t * W : (t + 1) * W, b * 2 * CS : (b + 1) * 2 * CS] for t in range(2)], axis=1)
        for z in range(8):
            out_ref[2 * z + b] = block
    for j in range(TM):
        pltpu.make_async_copy(buffer.at[j], res_ref.at[j], sems.at[j]).wait()


def subgrid_call(live, parts, vis):
    return pl.pallas_call(
        subgrid_kernel,
        in_specs=[VMEM, VMEM, VMEM],
        out_specs=[HBM, VMEM],
        out_shape=[
            jax.ShapeDtypeStruct((TM, CH, TR, 2 * SG), bf16),
            jax.ShapeDtypeStruct((LS // 2, W, 4 * CS), bf16),
        ],
        scratch_shapes=[pltpu.VMEM((TM, CH, TR, 2 * SG), bf16), pltpu.SemaphoreType.DMA((TM,))],
        compiler_params=params(24),
        cost_estimate=pl.CostEstimate(flops=20 << 20, bytes_accessed=2 << 20, transcendentals=0),
        name="subgrid",
    )(live, parts, vis)


def back_kernel(tiles_ref, offsets_ref, h_ref, own_ref, other_ref, out_ref, rhs_ref, phase_ref):
    phase_table(phase_ref)
    total = LS * W
    left = (iota((8 * W, 8 * CS), 1) & (2 * CS - 1)) < CS
    for step in range(4):
        ref = own_ref if step < 2 else other_ref
        x = ref[step % 2 * 8 : step % 2 * 8 + 8].reshape(8 * W, 4 * CS).astype(f32)
        y = swapped(x)
        real, imag = phases(phase_ref, tiles_ref, offsets_ref, step * 8)
        both = jnp.concatenate([x, x * real - y * imag], axis=1)
        turned = jnp.concatenate([y, y * real + x * imag], axis=1)
        rhs_ref[step * 8 * W : (step + 1) * 8 * W, :] = both.astype(bf16)
        rhs_ref[total + step * 8 * W : total + (step + 1) * 8 * W, :] = jnp.where(left, turned, -turned).astype(bf16)
    dims = (((0,), (0,)), ((), ()))
    for step in range(2):
        at = step * 4 * PB
        out = lax.dot_general(h_ref[:, at : at + 4 * PB], rhs_ref[:total], dims, preferred_element_type=f32)
        out = out + lax.dot_general(h_ref[:, LP + at : LP + at + 4 * PB], rhs_ref[total:], dims, preferred_element_type=f32)
        out_ref[step * 4 : step * 4 + 4] = out.reshape(4, PB, 8 * CS).astype(bf16)


def back_call(tiles, offsets, h, own, other):
    return pl.pallas_call(
        back_kernel,
        in_specs=[SMEM, SMEM, VMEM, VMEM, VMEM],
        out_specs=VMEM,
        out_shape=jax.ShapeDtypeStruct((ROWS, PB, 8 * CS), bf16),
        scratch_shapes=[pltpu.VMEM((2 * LS * W, 8 * CS), bf16), pltpu.VMEM((2, SG + TR, 2 * CS), f32)],
        compiler_params=params(24),
        cost_estimate=pl.CostEstimate(flops=1 << 30, bytes_accessed=4 << 20, transcendentals=0),
        name="back",
    )(tiles, offsets, h, own, other)


def facets_kernel(parts_ref, out_ref, buffer, sems, lhs_ref, base_ref):
    steps = FP // QT
    column_start(base_ref)
    total = parts_ref[0].astype(f32)
    for r in range(1, ROWS):
        total = total + parts_ref[r].astype(f32)
    total = total.astype(bf16)
    for a in range(2):
        for t in range(2):
            at = (a * 2 + t) * 2 * CS
            lhs_ref[(t * 2 + a) * PB : (t * 2 + a + 1) * PB, :] = total[:, at : at + 2 * CS]

    def copy(i):
        return pltpu.make_async_copy(buffer.at[i], out_ref.at[:, :, :, pl.ds(pl.multiple_of(i * QT, QT), QT)], sems.at[i])

    def body(i, carry):
        out = jnp.dot(lhs_ref[...], column_block(base_ref, i), preferred_element_type=f32)
        buffer[i] = out.reshape(2, 2, PB, QT).astype(bf16)
        copy(i).start()
        return carry

    lax.fori_loop(0, steps, body, 0)
    for i in range(steps):
        copy(i).wait()


def facets_call(parts):
    steps = FP // QT
    return pl.pallas_call(
        facets_kernel,
        in_specs=[VMEM],
        out_specs=HBM,
        out_shape=jax.ShapeDtypeStruct((2, 2, PB, FP), bf16),
        scratch_shapes=[
            pltpu.VMEM((steps, 2, 2, PB, QT), bf16),
            pltpu.SemaphoreType.DMA((steps,)),
            pltpu.VMEM((4 * PB, 2 * CS), bf16),
            pltpu.VMEM((6, 8, QT), f32),
        ],
        compiler_params=params(24),
        cost_estimate=pl.CostEstimate(flops=2 * 256 * 128 * FP, bytes_accessed=5 << 20, transcendentals=0),
        name="facets",
    )(parts)


def local(facet_model, sub_offsets, tile_rows, tile_counts, visibilities):
    rows_line, grid_line, all_line = ("xh", "y"), ("zh", "zl", "sub"), ("zh", "zl", "core", "sub")
    swap = [(0, 1), (1, 0)]

    def exchange(x, axes):
        return lax.all_to_all(x, axes, split_axis=0, concat_axis=0, tiled=True)

    tiles = exchange(jnp.broadcast_to(tile_rows, (LS, TM)), all_line)
    strips = exchange(strips_call(facet_model), rows_line)
    h, live = operator_call(tiles, sub_offsets, tile_counts, waves_call())

    own, other = fore_call(tiles, sub_offsets, h, strips)
    other = lax.ppermute(other, "core", swap)
    parts = exchange(add_call(own, other), grid_line)
    residual, back = subgrid_call(live, parts, visibilities[0])
    own = exchange(back, grid_line)
    other = lax.ppermute(own, "core", swap)
    sums = exchange(back_call(tiles, sub_offsets, h, own, other), rows_line)
    return facets_call(sums), residual[None]


def solution(mesh):
    split = Mesh(mesh.devices.reshape(4, 2, 2, 2, 4, 2), ("zh", "zl", "core", "xh", "y", "sub"))
    whole = ("zh", "zl", "core", "xh", "y", "sub")
    model = P(None, "sub", ("zh", "zl", "core", "xh", "y"), None)
    return jax.shard_map(
        local,
        mesh=split,
        in_specs=(model, P(), P(whole, None), P(whole), P(whole, None, None, None, None)),
        out_specs=(model, P(whole, None, None, None, None)),
        check_vma=False,
    )
```

```python
import math

import jax
import jax.numpy as jnp
from jax import lax
from jax.experimental import pallas as pl
from jax.experimental.pallas import tpu as pltpu
from jax.sharding import Mesh
from jax.sharding import PartitionSpec as P

SKY = 65536
FP = 8192
CS = 64
SG = 128
TM = 4
TR = 8
CH = 32
W = TM * TR
PB = 64
ROWS = 8
LP = ROWS * PB
LS = 32
QT = 1024

f32 = jnp.float32
bf16 = jnp.bfloat16


def turn(index, period):
    quarter = period // 4
    quadrant = lax.shift_right_logical(index + quarter // 2, quarter.bit_length() - 1)
    x = (index - quadrant * quarter).astype(f32) * (2.0 * math.pi / period)
    y = x * x
    sine = x * (1.0 + y * (-1.0 / 6 + y * (1.0 / 120 + y * (-1.0 / 5040 + y * (1.0 / 362880)))))
    cosine = 1.0 + y * (-0.5 + y * (1.0 / 24 + y * (-1.0 / 720 + y * (1.0 / 40320 - y * (1.0 / 3628800)))))
    swap = (quadrant & 1) == 1
    first = jnp.where(swap, sine, cosine)
    second = jnp.where(swap, cosine, sine)
    first = jnp.where(((quadrant + 1) & 2) == 2, -first, first)
    second = jnp.where((quadrant & 2) == 2, -second, second)
    return first, second


def taper(place):
    cosine, _ = turn(2 * place + 1, 2 * FP)
    return 0.625 - 0.375 * cosine


def iota(shape, dim):
    return lax.broadcasted_iota(jnp.int32, shape, dim)


def column_start(base_ref):
    place = iota((8, QT), 1)
    line = iota((8, QT), 0)
    tables = turn((line * place) & (QT - 1), QT) + turn((line * place) & (FP - 1), FP) + turn(2 * place + 1, 2 * FP)
    for i, table in enumerate(tables):
        base_ref[i] = table


def column_block(base_ref, step):
    wide = lambda x: jnp.concatenate([x] * (QT // 128), axis=1)
    move_re, move_im = (wide(x) for x in turn((iota((8, 128), 0) * step) & 7, 8))
    tilt_re, tilt_im = (wide(x) for x in turn(jnp.full((8, 128), step, jnp.int32), 8))
    cosine = base_ref[4] * tilt_re - base_ref[5] * tilt_im
    scale = (0.625 - 0.375 * cosine) * (1.0 / math.sqrt(FP))
    low_re = (base_ref[2] * move_re - base_ref[3] * move_im) * scale
    low_im = (base_ref[2] * move_im + base_ref[3] * move_re) * scale
    real, imag = [], []
    for k in range(8):
        re, im = base_ref[0, k : k + 1], base_ref[1, k : k + 1]
        real.append(low_re * re - low_im * im)
        imag.append(-(low_re * im + low_im * re))
    return jnp.concatenate(real + imag, axis=0).astype(bf16)


def subgrid_of(g):
    core = lax.axis_index("core")
    o, z, b = g // 16, (g // 2) % 8, g % 2
    c = core + o - 2 * core * o
    facet = z * 2 + c
    return facet * 2 + b, 2 * (facet * 8 + lax.axis_index("xh") * 4 + lax.axis_index("y")) + b


def line_rows(shape):
    z = lax.axis_index("zh") * 2 + lax.axis_index("zl")
    return (z * 2 + lax.axis_index("core")) * LP + iota(shape, 1)


def phase_table(ref):
    shape = (SG + TR, 2 * CS)
    cosine, sine = turn(iota(shape, 0) & (SG - 1), SG)
    ref[...] = jnp.where(iota(shape, 1) < CS, cosine, sine)


def factors(ref, step):
    x = ref[step * 8 * W : (step + 1) * 8 * W, :].astype(f32)
    y = pltpu.roll(x, CS, 1)
    left = iota(x.shape, 1) < CS
    real = jnp.where(left, x, y)
    imag = jnp.where(left, -y, x)
    return jnp.concatenate([real, real], axis=1), jnp.concatenate([imag, imag], axis=1)


def swapped(x):
    return jnp.concatenate([pltpu.roll(x[:, i : i + 2 * CS], CS, 1) for i in range(0, x.shape[1], 2 * CS)], axis=1)


SMEM = pl.BlockSpec(memory_space=pltpu.SMEM)
VMEM = pl.BlockSpec(memory_space=pltpu.VMEM)
HBM = pl.BlockSpec(memory_space=pltpu.HBM)


def params(mib):
    return pltpu.CompilerParams(vmem_limit_bytes=mib << 20)


def strips_kernel(model_ref, out_ref, buffer, sems, base_ref, table_ref):
    rows = PB // 2

    def copy(i):
        return pltpu.make_async_copy(
            model_ref.at[i // 4, (i // 2) % 2, pl.ds((i % 2) * rows, rows), :], buffer.at[i], sems.at[i]
        )

    for i in range(8):
        copy(i).start()
    column_start(base_ref)

    def body(i, carry):
        table_ref[:, pl.ds(pl.multiple_of(i * QT, QT), QT)] = column_block(base_ref, i)
        return carry

    lax.fori_loop(0, FP // QT, body, 0)
    for i in range(8):
        copy(i).wait()
    strips = lax.dot_general(
        buffer[...].reshape(4 * PB, FP), table_ref[...], (((1,), (1,)), ((), ())), preferred_element_type=f32
    ).astype(bf16)
    parts = [strips[(t * 2 + a) * PB : (t * 2 + a + 1) * PB] for a in range(2) for t in range(2)]
    strip = jnp.concatenate(parts, axis=1)
    for r in range(ROWS):
        out_ref[r] = strip


def strips_call(model):
    return pl.pallas_call(
        strips_kernel,
        in_specs=[HBM],
        out_specs=VMEM,
        out_shape=jax.ShapeDtypeStruct((ROWS, PB, 8 * CS), bf16),
        scratch_shapes=[
            pltpu.VMEM((8, PB // 2, FP), bf16),
            pltpu.SemaphoreType.DMA((8,)),
            pltpu.VMEM((6, 8, QT), f32),
            pltpu.VMEM((2 * CS, FP), bf16),
        ],
        compiler_params=params(60),
        cost_estimate=pl.CostEstimate(flops=2 * 256 * 128 * FP, bytes_accessed=5 << 20, transcendentals=0),
        name="strips",
    )(model)


def waves_kernel(d_ref):
    p = line_rows((TR, LP))
    line = iota((TR, LP), 0)

    def body(i, carry):
        n = (SG * (i * TR + line) - p) & (FP - 1)
        _, under = turn(n, 2 * FP)
        _, over = turn((CS * n) & (2 * FP - 1), 2 * FP)
        ratio = jnp.where(n == 0, float(CS), over / jnp.where(n == 0, 1.0, under))
        re, im = turn(((CS - 1) * n) & (2 * FP - 1), 2 * FP)
        for c, part in enumerate((re * ratio, im * ratio)):
            for q in range(LP // 128):
                d_ref[c, q, pl.ds(pl.multiple_of(i * TR, TR), TR), :] = part[:, q * 128 : (q + 1) * 128]
        return carry

    lax.fori_loop(0, SG // TR, body, 0)


def waves_call():
    return pl.pallas_call(
        waves_kernel,
        out_specs=VMEM,
        out_shape=jax.ShapeDtypeStruct((2, LP // 128, SG, 128), f32),
        compiler_params=params(24),
        cost_estimate=pl.CostEstimate(flops=8 << 20, bytes_accessed=1 << 20, transcendentals=0),
        name="waves",
    )()


def operator_kernel(
    tiles_ref, offsets_ref, count_ref, d_ref, h_ref, live_ref, factor_ref, table_ref, e_ref, phase_ref, buffer, sems, base_ref
):
    def copy(i):
        return pltpu.make_async_copy(buffer.at[i], table_ref.at[:, pl.ds(pl.multiple_of(i * QT, QT), QT)], sems.at[i])

    def block(i, carry):
        buffer[i] = column_block(base_ref, i)
        copy(i).start()
        return carry

    column_start(base_ref)
    lax.fori_loop(0, FP // QT, block, 0)
    phase_table(phase_ref)
    live_ref[...] = jnp.where(iota((W, 128), 0) < TR * count_ref[0], 1.0, 0.0)
    place = line_rows((8, LP))
    line = iota((8, LP), 0)
    scale = taper(place) * (1.0 / 1024)

    def body(step, carry):
        offset = jnp.zeros((8, LP), jnp.int32)
        index, offs = [], []
        for i in range(8):
            at, s = subgrid_of(step * 8 + i)
            index.append(at)
            offs.append(offsets_ref[s])
            offset = jnp.where(line == i, offsets_ref[s], offset)
        cosine, sine = turn((offset * place) & (SKY - 1), SKY)
        e_ref[0] = cosine * scale
        e_ref[1] = -sine * scale
        for half in range(2):
            real, imag, factor = [], [], []
            for i in range(4 * half, 4 * half + 4):
                er = e_ref[0, i : i + 1, :]
                ei = e_ref[1, i : i + 1, :]
                for j in range(TM):
                    at = tiles_ref[index[i], j]
                    n = (at - 16 * offs[i]) & (SG - 1)
                    factor.append(phase_ref[pl.ds(n, TR), :])
                    dr = jnp.concatenate([d_ref[0, q, pl.ds(at, TR), :] for q in range(LP // 128)], axis=1)
                    di = jnp.concatenate([d_ref[1, q, pl.ds(at, TR), :] for q in range(LP // 128)], axis=1)
                    real.append(dr * er - di * ei)
                    imag.append(dr * ei + di * er)
            rows = pl.ds(pl.multiple_of(step * 8 * W + half * 4 * W, 4 * W), 4 * W)
            h_ref[rows, :LP] = jnp.concatenate(real, axis=0).astype(bf16)
            h_ref[rows, LP:] = jnp.concatenate(imag, axis=0).astype(bf16)
            factor_ref[rows, :] = jnp.concatenate(factor, axis=0).astype(bf16)
        return carry

    lax.fori_loop(0, LS // 8, body, 0)
    for i in range(FP // QT):
        copy(i).wait()


def operator_call(tiles, offsets, count, waves):
    return pl.pallas_call(
        operator_kernel,
        in_specs=[SMEM, SMEM, SMEM, VMEM],
        out_specs=[VMEM, VMEM, VMEM, HBM],
        out_shape=[
            jax.ShapeDtypeStruct((LS * W, 2 * LP), bf16),
            jax.ShapeDtypeStruct((W, 128), f32),
            jax.ShapeDtypeStruct((LS * W, 2 * CS), bf16),
            pltpu.HBM((2 * CS, FP), bf16),
        ],
        scratch_shapes=[
            pltpu.VMEM((2, 8, LP), f32),
            pltpu.VMEM((SG + TR, 2 * CS), f32),
            pltpu.VMEM((FP // QT, 2 * CS, QT), bf16),
            pltpu.SemaphoreType.DMA((FP // QT,)),
            pltpu.VMEM((6, 8, QT), f32),
        ],
        compiler_params=params(24),
        cost_estimate=pl.CostEstimate(flops=20 << 20, bytes_accessed=8 << 20, transcendentals=0),
        name="operator",
    )(tiles, offsets, count, waves)


def fore_kernel(factor_ref, h_ref, strips_ref, own_ref, other_ref, rhs_ref):
    left = iota((PB, 2 * CS), 1) < CS
    for r in range(ROWS):
        strips = strips_ref[r]
        rhs_ref[r * PB : (r + 1) * PB, :] = strips
        for at in range(0, 8 * CS, 2 * CS):
            turned = pltpu.roll(strips[:, at : at + 2 * CS].astype(f32), CS, 1)
            rhs_ref[LP + r * PB : LP + (r + 1) * PB, at : at + 2 * CS] = jnp.where(left, -turned, turned).astype(bf16)
    rows = 8 * W
    for step in range(4):
        out = jnp.dot(h_ref[step * rows : (step + 1) * rows, :], rhs_ref[...], preferred_element_type=f32)
        real, imag = factors(factor_ref, step)
        second = out[:, 4 * CS :]
        out = out[:, : 4 * CS] + second * real + swapped(second) * imag
        ref = own_ref if step < 2 else other_ref
        ref[step % 2 * 8 : step % 2 * 8 + 8] = out.reshape(8, W, 4 * CS).astype(bf16)


def fore_call(factor, h, strips):
    return pl.pallas_call(
        fore_kernel,
        in_specs=[VMEM, VMEM, VMEM],
        out_specs=[VMEM, VMEM],
        out_shape=[jax.ShapeDtypeStruct((LS // 2, W, 4 * CS), bf16)] * 2,
        scratch_shapes=[pltpu.VMEM((2 * LP, 8 * CS), bf16)],
        compiler_params=params(24),
        cost_estimate=pl.CostEstimate(flops=1 << 30, bytes_accessed=4 << 20, transcendentals=0),
        name="fore",
    )(factor, h, strips)


def add_kernel(own_ref, other_ref, out_ref):
    out_ref[...] = (own_ref[...].astype(f32) + other_ref[...].astype(f32)).astype(bf16)


def add_call(own, other):
    return pl.pallas_call(
        add_kernel,
        in_specs=[VMEM, VMEM],
        out_specs=VMEM,
        out_shape=jax.ShapeDtypeStruct(own.shape, bf16),
        compiler_params=params(24),
        cost_estimate=pl.CostEstimate(flops=1 << 18, bytes_accessed=1 << 20, transcendentals=0),
        name="add",
    )(own, other)


def subgrid_kernel(live_ref, parts_ref, vis_ref, res_ref, out_ref, buffer, sems):
    l = iota((2 * CS, SG), 0) & (CS - 1)
    upper = iota((2 * CS, SG), 0) < CS
    v = iota((2 * CS, SG), 1)
    rows = []
    for b in range(2):
        cosine, sine = turn((v * (2 * l + b)) & (SG - 1), SG)
        real = jnp.where(upper, cosine, -sine)
        imag = jnp.where(upper, sine, cosine)
        rows.append(jnp.concatenate([real, imag], axis=1))
    table = (jnp.concatenate(rows, axis=0) * (1.0 / math.sqrt(SG))).astype(bf16)

    fronts = []
    for b in range(2):
        total = parts_ref[b].astype(f32)
        for z in range(1, 8):
            total = total + parts_ref[2 * z + b].astype(f32)
        fronts.append(total.astype(bf16))
    front = jnp.concatenate(
        [jnp.concatenate([fronts[b][:, t * 2 * CS : (t + 1) * 2 * CS] for b in range(2)], axis=1) for t in range(2)],
        axis=0,
    )
    sky = jnp.dot(front, table, preferred_element_type=f32).astype(bf16).astype(f32)
    weighted = [[], []]
    for j in range(TM):
        m0 = sky[j * TR : (j + 1) * TR]
        m1 = sky[W + j * TR : W + (j + 1) * TR]
        live = live_ref[j * TR : (j + 1) * TR, :]
        live = jnp.concatenate([live, live], axis=1)
        w0 = jnp.zeros((TR, 2 * SG), f32)
        w1 = jnp.zeros((TR, 2 * SG), f32)
        for c in range(CH):
            nu = (c + 0.5) / CH - 0.5
            res = (vis_ref[j, c].astype(f32) - (m0 + nu * m1)) * live
            buffer[j, c] = res.astype(bf16)
            w0 = w0 + res
            w1 = w1 + nu * res
        pltpu.make_async_copy(buffer.at[j], res_ref.at[j], sems.at[j]).start()
        weighted[0].append(w0)
        weighted[1].append(w1)
    weight = jnp.concatenate(weighted[0] + weighted[1], axis=0).astype(bf16)
    back = lax.dot_general(weight, table, (((1,), (1,)), ((), ())), preferred_element_type=f32).astype(bf16)
    for b in range(2):
        block = jnp.concatenate([back[t * W : (t + 1) * W, b * 2 * CS : (b + 1) * 2 * CS] for t in range(2)], axis=1)
        for z in range(8):
            out_ref[2 * z + b] = block
    for j in range(TM):
        pltpu.make_async_copy(buffer.at[j], res_ref.at[j], sems.at[j]).wait()


def subgrid_call(live, parts, vis):
    return pl.pallas_call(
        subgrid_kernel,
        in_specs=[VMEM, VMEM, VMEM],
        out_specs=[HBM, VMEM],
        out_shape=[
            jax.ShapeDtypeStruct((TM, CH, TR, 2 * SG), bf16),
            jax.ShapeDtypeStruct((LS // 2, W, 4 * CS), bf16),
        ],
        scratch_shapes=[pltpu.VMEM((TM, CH, TR, 2 * SG), bf16), pltpu.SemaphoreType.DMA((TM,))],
        compiler_params=params(24),
        cost_estimate=pl.CostEstimate(flops=20 << 20, bytes_accessed=2 << 20, transcendentals=0),
        name="subgrid",
    )(live, parts, vis)


def back_kernel(factor_ref, h_ref, own_ref, other_ref, out_ref, rhs_ref):
    total = LS * W
    left = (iota((8 * W, 8 * CS), 1) & (2 * CS - 1)) < CS
    for step in range(4):
        ref = own_ref if step < 2 else other_ref
        x = ref[step % 2 * 8 : step % 2 * 8 + 8].reshape(8 * W, 4 * CS).astype(f32)
        y = swapped(x)
        real, imag = factors(factor_ref, step)
        both = jnp.concatenate([x, x * real - y * imag], axis=1)
        turned = jnp.concatenate([y, y * real + x * imag], axis=1)
        rhs_ref[step * 8 * W : (step + 1) * 8 * W, :] = both.astype(bf16)
        rhs_ref[total + step * 8 * W : total + (step + 1) * 8 * W, :] = jnp.where(left, turned, -turned).astype(bf16)
    dims = (((0,), (0,)), ((), ()))
    for step in range(2):
        at = step * 4 * PB
        out = lax.dot_general(h_ref[:, at : at + 4 * PB], rhs_ref[:total], dims, preferred_element_type=f32)
        out = out + lax.dot_general(h_ref[:, LP + at : LP + at + 4 * PB], rhs_ref[total:], dims, preferred_element_type=f32)
        out_ref[step * 4 : step * 4 + 4] = out.reshape(4, PB, 8 * CS).astype(bf16)


def back_call(factor, h, own, other):
    return pl.pallas_call(
        back_kernel,
        in_specs=[VMEM, VMEM, VMEM, VMEM],
        out_specs=VMEM,
        out_shape=jax.ShapeDtypeStruct((ROWS, PB, 8 * CS), bf16),
        scratch_shapes=[pltpu.VMEM((2 * LS * W, 8 * CS), bf16)],
        compiler_params=params(24),
        cost_estimate=pl.CostEstimate(flops=1 << 30, bytes_accessed=4 << 20, transcendentals=0),
        name="back",
    )(factor, h, own, other)


def facets_kernel(parts_ref, table_ref, out_ref, buffer, sems, lhs_ref):
    steps = FP // QT
    total = parts_ref[0].astype(f32)
    for r in range(1, ROWS):
        total = total + parts_ref[r].astype(f32)
    total = total.astype(bf16)
    for a in range(2):
        for t in range(2):
            at = (a * 2 + t) * 2 * CS
            lhs_ref[(t * 2 + a) * PB : (t * 2 + a + 1) * PB, :] = total[:, at : at + 2 * CS]

    def copy(i):
        return pltpu.make_async_copy(buffer.at[i], out_ref.at[:, :, :, pl.ds(pl.multiple_of(i * QT, QT), QT)], sems.at[i])

    def body(i, carry):
        table = table_ref[:, pl.ds(pl.multiple_of(i * QT, QT), QT)]
        out = jnp.dot(lhs_ref[...], table, preferred_element_type=f32)
        buffer[i] = out.reshape(2, 2, PB, QT).astype(bf16)
        copy(i).start()
        return carry

    lax.fori_loop(0, steps, body, 0)
    for i in range(steps):
        copy(i).wait()


def facets_call(parts, table):
    steps = FP // QT
    return pl.pallas_call(
        facets_kernel,
        in_specs=[VMEM, VMEM],
        out_specs=HBM,
        out_shape=jax.ShapeDtypeStruct((2, 2, PB, FP), bf16),
        scratch_shapes=[
            pltpu.VMEM((steps, 2, 2, PB, QT), bf16),
            pltpu.SemaphoreType.DMA((steps,)),
            pltpu.VMEM((4 * PB, 2 * CS), bf16),
        ],
        compiler_params=params(24),
        cost_estimate=pl.CostEstimate(flops=2 * 256 * 128 * FP, bytes_accessed=5 << 20, transcendentals=0),
        name="facets",
    )(parts, table)


def local(facet_model, sub_offsets, tile_rows, tile_counts, visibilities):
    rows_line, grid_line, all_line = ("xh", "y"), ("zh", "zl", "sub"), ("zh", "zl", "core", "sub")
    swap = [(0, 1), (1, 0)]

    def exchange(x, axes):
        return lax.all_to_all(x, axes, split_axis=0, concat_axis=0, tiled=True)

    tiles = exchange(jnp.broadcast_to(tile_rows, (LS, TM)), all_line)
    strips = exchange(strips_call(facet_model), rows_line)
    h, live, factor, table = operator_call(tiles, sub_offsets, tile_counts, waves_call())

    own, other = fore_call(factor, h, strips)
    other = lax.ppermute(other, "core", swap)
    parts = exchange(add_call(own, other), grid_line)
    residual, back = subgrid_call(live, parts, visibilities[0])
    own = exchange(back, grid_line)
    other = lax.ppermute(own, "core", swap)
    sums = exchange(back_call(factor, h, own, other), rows_line)
    return facets_call(sums, table), residual[None]


def solution(mesh):
    split = Mesh(mesh.devices.reshape(4, 2, 2, 2, 4, 2), ("zh", "zl", "core", "xh", "y", "sub"))
    whole = ("zh", "zl", "core", "xh", "y", "sub")
    model = P(None, "sub", ("zh", "zl", "core", "xh", "y"), None)
    return jax.shard_map(
        local,
        mesh=split,
        in_specs=(model, P(), P(whole, None), P(whole), P(whole, None, None, None, None)),
        out_specs=(model, P(whole, None, None, None, None)),
        check_vma=False,
    )
```

```python
import math

import jax
import jax.numpy as jnp
from jax import lax
from jax.experimental import pallas as pl
from jax.experimental.pallas import tpu as pltpu
from jax.sharding import Mesh
from jax.sharding import PartitionSpec as P

SKY = 65536
FP = 8192
CS = 64
SG = 128
TM = 4
TR = 8
CH = 32
W = TM * TR
PB = 64
ROWS = 8
LP = ROWS * PB
LS = 32
QT = 1024

f32 = jnp.float32
bf16 = jnp.bfloat16


def turn(index, period):
    quarter = period // 4
    quadrant = lax.shift_right_logical(index + quarter // 2, quarter.bit_length() - 1)
    x = (index - quadrant * quarter).astype(f32) * (2.0 * math.pi / period)
    y = x * x
    sine = x * (1.0 + y * (-1.0 / 6 + y * (1.0 / 120 + y * (-1.0 / 5040 + y * (1.0 / 362880)))))
    cosine = 1.0 + y * (-0.5 + y * (1.0 / 24 + y * (-1.0 / 720 + y * (1.0 / 40320 - y * (1.0 / 3628800)))))
    swap = (quadrant & 1) == 1
    first = jnp.where(swap, sine, cosine)
    second = jnp.where(swap, cosine, sine)
    first = jnp.where(((quadrant + 1) & 2) == 2, -first, first)
    second = jnp.where((quadrant & 2) == 2, -second, second)
    return first, second


def taper(place):
    cosine, _ = turn(2 * place + 1, 2 * FP)
    return 0.625 - 0.375 * cosine


def iota(shape, dim):
    return lax.broadcasted_iota(jnp.int32, shape, dim)


def column_start(base_ref):
    place = iota((8, QT), 1)
    line = iota((8, QT), 0)
    tables = turn((line * place) & (QT - 1), QT) + turn((line * place) & (FP - 1), FP) + turn(2 * place + 1, 2 * FP)
    for i, table in enumerate(tables):
        base_ref[i] = table


def column_block(base_ref, step):
    wide = lambda x: jnp.concatenate([x] * (QT // 128), axis=1)
    move_re, move_im = (wide(x) for x in turn((iota((8, 128), 0) * step) & 7, 8))
    tilt_re, tilt_im = (wide(x) for x in turn(jnp.full((8, 128), step, jnp.int32), 8))
    cosine = base_ref[4] * tilt_re - base_ref[5] * tilt_im
    scale = (0.625 - 0.375 * cosine) * (1.0 / math.sqrt(FP))
    low_re = (base_ref[2] * move_re - base_ref[3] * move_im) * scale
    low_im = (base_ref[2] * move_im + base_ref[3] * move_re) * scale
    real, imag = [], []
    for k in range(8):
        re, im = base_ref[0, k : k + 1], base_ref[1, k : k + 1]
        real.append(low_re * re - low_im * im)
        imag.append(-(low_re * im + low_im * re))
    return jnp.concatenate(real + imag, axis=0).astype(bf16)


def subgrid_of(g):
    core = lax.axis_index("core")
    o, z, b = g // 16, (g // 2) % 8, g % 2
    c = core + o - 2 * core * o
    facet = z * 2 + c
    return facet * 2 + b, 2 * (facet * 8 + lax.axis_index("xh") * 4 + lax.axis_index("y")) + b


def line_rows(shape):
    z = lax.axis_index("zh") * 2 + lax.axis_index("zl")
    return (z * 2 + lax.axis_index("core")) * LP + iota(shape, 1)


def phase_table(ref):
    shape = (SG + TR, 2 * CS)
    cosine, sine = turn(iota(shape, 0) & (SG - 1), SG)
    ref[...] = jnp.where(iota(shape, 1) < CS, cosine, sine)


def factors(ref, step):
    x = ref[step * 8 * W : (step + 1) * 8 * W, :].astype(f32)
    y = pltpu.roll(x, CS, 1)
    left = iota(x.shape, 1) < CS
    real = jnp.where(left, x, y)
    imag = jnp.where(left, -y, x)
    return jnp.concatenate([real, real], axis=1), jnp.concatenate([imag, imag], axis=1)


def swapped(x):
    return jnp.concatenate([pltpu.roll(x[:, i : i + 2 * CS], CS, 1) for i in range(0, x.shape[1], 2 * CS)], axis=1)


SMEM = pl.BlockSpec(memory_space=pltpu.SMEM)
VMEM = pl.BlockSpec(memory_space=pltpu.VMEM)
HBM = pl.BlockSpec(memory_space=pltpu.HBM)


def params(mib):
    return pltpu.CompilerParams(vmem_limit_bytes=mib << 20)


def strips_kernel(model_ref, out_ref, buffer, sems, base_ref, table_ref):
    rows = PB // 2

    def copy(i):
        return pltpu.make_async_copy(
            model_ref.at[i // 4, (i // 2) % 2, pl.ds((i % 2) * rows, rows), :], buffer.at[i], sems.at[i]
        )

    for i in range(8):
        copy(i).start()
    column_start(base_ref)

    def body(i, carry):
        table_ref[:, pl.ds(pl.multiple_of(i * QT, QT), QT)] = column_block(base_ref, i)
        return carry

    lax.fori_loop(0, FP // QT, body, 0)
    for i in range(8):
        copy(i).wait()
    strips = lax.dot_general(
        buffer[...].reshape(4 * PB, FP), table_ref[...], (((1,), (1,)), ((), ())), preferred_element_type=f32
    ).astype(bf16)
    parts = [strips[(t * 2 + a) * PB : (t * 2 + a + 1) * PB] for a in range(2) for t in range(2)]
    strip = jnp.concatenate(parts, axis=1)
    for r in range(ROWS):
        out_ref[r] = strip


def strips_call(model):
    return pl.pallas_call(
        strips_kernel,
        in_specs=[HBM],
        out_specs=VMEM,
        out_shape=jax.ShapeDtypeStruct((ROWS, PB, 8 * CS), bf16),
        scratch_shapes=[
            pltpu.VMEM((8, PB // 2, FP), bf16),
            pltpu.SemaphoreType.DMA((8,)),
            pltpu.VMEM((6, 8, QT), f32),
            pltpu.VMEM((2 * CS, FP), bf16),
        ],
        compiler_params=params(60),
        cost_estimate=pl.CostEstimate(flops=2 * 256 * 128 * FP, bytes_accessed=5 << 20, transcendentals=0),
        name="strips",
    )(model)


def waves_kernel(d_ref):
    p = line_rows((TR, LP))
    line = iota((TR, LP), 0)

    def body(i, carry):
        n = (SG * (i * TR + line) - p) & (FP - 1)
        _, under = turn(n, 2 * FP)
        _, over = turn((CS * n) & (2 * FP - 1), 2 * FP)
        ratio = jnp.where(n == 0, float(CS), over / jnp.where(n == 0, 1.0, under))
        re, im = turn(((CS - 1) * n) & (2 * FP - 1), 2 * FP)
        for c, part in enumerate((re * ratio, im * ratio)):
            for q in range(LP // 128):
                d_ref[c, q, pl.ds(pl.multiple_of(i * TR, TR), TR), :] = part[:, q * 128 : (q + 1) * 128]
        return carry

    lax.fori_loop(0, SG // TR, body, 0)


def waves_call():
    return pl.pallas_call(
        waves_kernel,
        out_specs=VMEM,
        out_shape=jax.ShapeDtypeStruct((2, LP // 128, SG, 128), f32),
        compiler_params=params(24),
        cost_estimate=pl.CostEstimate(flops=8 << 20, bytes_accessed=1 << 20, transcendentals=0),
        name="waves",
    )()


def operator_kernel(
    tiles_ref, offsets_ref, count_ref, d_ref, h_ref, live_ref, factor_ref, table_ref, e_ref, phase_ref, buffer, sems, base_ref
):
    def copy(i):
        return pltpu.make_async_copy(buffer.at[i], table_ref.at[:, pl.ds(pl.multiple_of(i * QT, QT), QT)], sems.at[i])

    def block(i, carry):
        buffer[i] = column_block(base_ref, i)
        copy(i).start()
        return carry

    column_start(base_ref)
    lax.fori_loop(0, FP // QT, block, 0)
    phase_table(phase_ref)
    live_ref[...] = jnp.where(iota((W, 128), 0) < TR * count_ref[0], 1.0, 0.0)
    place = line_rows((8, LP))
    line = iota((8, LP), 0)
    scale = taper(place) * (1.0 / 1024)

    def body(step, carry):
        offset = jnp.zeros((8, LP), jnp.int32)
        index, offs = [], []
        for i in range(8):
            at, s = subgrid_of(step * 8 + i)
            index.append(at)
            offs.append(offsets_ref[s])
            offset = jnp.where(line == i, offsets_ref[s], offset)
        cosine, sine = turn((offset * place) & (SKY - 1), SKY)
        e_ref[0] = cosine * scale
        e_ref[1] = -sine * scale
        for half in range(2):
            real, imag, factor = [], [], []
            for i in range(4 * half, 4 * half + 4):
                er = e_ref[0, i : i + 1, :]
                ei = e_ref[1, i : i + 1, :]
                for j in range(TM):
                    at = tiles_ref[index[i], j]
                    n = (at - 16 * offs[i]) & (SG - 1)
                    factor.append(phase_ref[pl.ds(n, TR), :])
                    dr = jnp.concatenate([d_ref[0, q, pl.ds(at, TR), :] for q in range(LP // 128)], axis=1)
                    di = jnp.concatenate([d_ref[1, q, pl.ds(at, TR), :] for q in range(LP // 128)], axis=1)
                    real.append(dr * er - di * ei)
                    imag.append(dr * ei + di * er)
            rows = pl.ds(pl.multiple_of(step * 8 * W + half * 4 * W, 4 * W), 4 * W)
            h_ref[rows, :LP] = jnp.concatenate(real, axis=0).astype(bf16)
            h_ref[rows, LP:] = jnp.concatenate(imag, axis=0).astype(bf16)
            factor_ref[rows, :] = jnp.concatenate(factor, axis=0).astype(bf16)
        return carry

    lax.fori_loop(0, LS // 8, body, 0)
    for i in range(FP // QT):
        copy(i).wait()


def operator_call(tiles, offsets, count, waves):
    return pl.pallas_call(
        operator_kernel,
        in_specs=[SMEM, SMEM, SMEM, VMEM],
        out_specs=[VMEM, VMEM, VMEM, HBM],
        out_shape=[
            jax.ShapeDtypeStruct((LS * W, 2 * LP), bf16),
            jax.ShapeDtypeStruct((W, 128), f32),
            jax.ShapeDtypeStruct((LS * W, 2 * CS), bf16),
            pltpu.HBM((2 * CS, FP), bf16),
        ],
        scratch_shapes=[
            pltpu.VMEM((2, 8, LP), f32),
            pltpu.VMEM((SG + TR, 2 * CS), f32),
            pltpu.VMEM((FP // QT, 2 * CS, QT), bf16),
            pltpu.SemaphoreType.DMA((FP // QT,)),
            pltpu.VMEM((6, 8, QT), f32),
        ],
        compiler_params=params(24),
        cost_estimate=pl.CostEstimate(flops=20 << 20, bytes_accessed=8 << 20, transcendentals=0),
        name="operator",
    )(tiles, offsets, count, waves)


HALF = jax.ShapeDtypeStruct((LS // 2, W, 4 * CS), bf16)


def fore_half(factor_ref, h_ref, rhs_ref, o, put):
    rows = 8 * W
    for q in range(2):
        step = 2 * o + q
        out = jnp.dot(h_ref[step * rows : (step + 1) * rows, :], rhs_ref[...], preferred_element_type=f32)
        real, imag = factors(factor_ref, step)
        second = out[:, 4 * CS :]
        out = out[:, : 4 * CS] + second * real + swapped(second) * imag
        put(slice(q * 8, q * 8 + 8), out.reshape(8, W, 4 * CS))


def fore_other_kernel(factor_ref, h_ref, strips_ref, out_ref, rhs_ref):
    left = iota((PB, 2 * CS), 1) < CS
    for r in range(ROWS):
        strips = strips_ref[r]
        rhs_ref[r * PB : (r + 1) * PB, :] = strips
        for at in range(0, 8 * CS, 2 * CS):
            turned = pltpu.roll(strips[:, at : at + 2 * CS].astype(f32), CS, 1)
            rhs_ref[LP + r * PB : LP + (r + 1) * PB, at : at + 2 * CS] = jnp.where(left, -turned, turned).astype(bf16)

    def put(at, out):
        out_ref[at] = out.astype(bf16)

    fore_half(factor_ref, h_ref, rhs_ref, 1, put)


def fore_own_kernel(factor_ref, h_ref, rhs_ref, out_ref):
    def put(at, out):
        out_ref[at] = out.astype(bf16)

    fore_half(factor_ref, h_ref, rhs_ref, 0, put)


def fore_other_call(factor, h, strips):
    return pl.pallas_call(
        fore_other_kernel,
        in_specs=[VMEM, VMEM, VMEM],
        out_specs=[VMEM, VMEM],
        out_shape=[HALF, jax.ShapeDtypeStruct((2 * LP, 8 * CS), bf16)],
        compiler_params=params(24),
        cost_estimate=pl.CostEstimate(flops=1 << 29, bytes_accessed=4 << 20, transcendentals=0),
        name="fore_other",
    )(factor, h, strips)


def fore_own_call(factor, h, rhs):
    return pl.pallas_call(
        fore_own_kernel,
        in_specs=[VMEM, VMEM, VMEM],
        out_specs=VMEM,
        out_shape=HALF,
        compiler_params=params(24),
        cost_estimate=pl.CostEstimate(flops=1 << 29, bytes_accessed=4 << 20, transcendentals=0),
        name="fore_own",
    )(factor, h, rhs)


def add_kernel(own_ref, other_ref, out_ref):
    out_ref[...] = (own_ref[...].astype(f32) + other_ref[...].astype(f32)).astype(bf16)


def add_call(own, other):
    return pl.pallas_call(
        add_kernel,
        in_specs=[VMEM, VMEM],
        out_specs=VMEM,
        out_shape=jax.ShapeDtypeStruct(own.shape, bf16),
        compiler_params=params(24),
        cost_estimate=pl.CostEstimate(flops=1 << 18, bytes_accessed=1 << 20, transcendentals=0),
        name="add",
    )(own, other)


def subgrid_kernel(live_ref, parts_ref, vis_ref, res_ref, out_ref, buffer, sems):
    l = iota((2 * CS, SG), 0) & (CS - 1)
    upper = iota((2 * CS, SG), 0) < CS
    v = iota((2 * CS, SG), 1)
    rows = []
    for b in range(2):
        cosine, sine = turn((v * (2 * l + b)) & (SG - 1), SG)
        real = jnp.where(upper, cosine, -sine)
        imag = jnp.where(upper, sine, cosine)
        rows.append(jnp.concatenate([real, imag], axis=1))
    table = (jnp.concatenate(rows, axis=0) * (1.0 / math.sqrt(SG))).astype(bf16)

    fronts = []
    for b in range(2):
        total = parts_ref[b].astype(f32)
        for z in range(1, 8):
            total = total + parts_ref[2 * z + b].astype(f32)
        fronts.append(total.astype(bf16))
    front = jnp.concatenate(
        [jnp.concatenate([fronts[b][:, t * 2 * CS : (t + 1) * 2 * CS] for b in range(2)], axis=1) for t in range(2)],
        axis=0,
    )
    sky = jnp.dot(front, table, preferred_element_type=f32).astype(bf16).astype(f32)
    weighted = [[], []]
    for j in range(TM):
        m0 = sky[j * TR : (j + 1) * TR]
        m1 = sky[W + j * TR : W + (j + 1) * TR]
        live = live_ref[j * TR : (j + 1) * TR, :]
        live = jnp.concatenate([live, live], axis=1)
        w0 = jnp.zeros((TR, 2 * SG), f32)
        w1 = jnp.zeros((TR, 2 * SG), f32)
        for c in range(CH):
            nu = (c + 0.5) / CH - 0.5
            res = (vis_ref[j, c].astype(f32) - (m0 + nu * m1)) * live
            buffer[j, c] = res.astype(bf16)
            w0 = w0 + res
            w1 = w1 + nu * res
        pltpu.make_async_copy(buffer.at[j], res_ref.at[j], sems.at[j]).start()
        weighted[0].append(w0)
        weighted[1].append(w1)
    weight = jnp.concatenate(weighted[0] + weighted[1], axis=0).astype(bf16)
    back = lax.dot_general(weight, table, (((1,), (1,)), ((), ())), preferred_element_type=f32).astype(bf16)
    for b in range(2):
        block = jnp.concatenate([back[t * W : (t + 1) * W, b * 2 * CS : (b + 1) * 2 * CS] for t in range(2)], axis=1)
        for z in range(8):
            out_ref[2 * z + b] = block
    for j in range(TM):
        pltpu.make_async_copy(buffer.at[j], res_ref.at[j], sems.at[j]).wait()


def subgrid_call(live, parts, vis):
    return pl.pallas_call(
        subgrid_kernel,
        in_specs=[VMEM, VMEM, VMEM],
        out_specs=[HBM, VMEM],
        out_shape=[
            jax.ShapeDtypeStruct((TM, CH, TR, 2 * SG), bf16),
            jax.ShapeDtypeStruct((LS // 2, W, 4 * CS), bf16),
        ],
        scratch_shapes=[pltpu.VMEM((TM, CH, TR, 2 * SG), bf16), pltpu.SemaphoreType.DMA((TM,))],
        compiler_params=params(24),
        cost_estimate=pl.CostEstimate(flops=20 << 20, bytes_accessed=2 << 20, transcendentals=0),
        name="subgrid",
    )(live, parts, vis)


def back_half(factor_ref, h_ref, x_ref, rhs_ref, o, put):
    left = (iota((8 * W, 8 * CS), 1) & (2 * CS - 1)) < CS
    total = LS * W // 2
    for q in range(2):
        x = x_ref[q * 8 : q * 8 + 8].reshape(8 * W, 4 * CS).astype(f32)
        y = swapped(x)
        real, imag = factors(factor_ref, 2 * o + q)
        both = jnp.concatenate([x, x * real - y * imag], axis=1)
        turned = jnp.concatenate([y, y * real + x * imag], axis=1)
        rhs_ref[q * 8 * W : (q + 1) * 8 * W, :] = both.astype(bf16)
        rhs_ref[total + q * 8 * W : total + (q + 1) * 8 * W, :] = jnp.where(left, turned, -turned).astype(bf16)
    dims = (((0,), (0,)), ((), ()))
    rows = slice(o * total, (o + 1) * total)
    for step in range(2):
        at = step * 4 * PB
        out = lax.dot_general(h_ref[rows, at : at + 4 * PB], rhs_ref[:total], dims, preferred_element_type=f32)
        out = out + lax.dot_general(h_ref[rows, LP + at : LP + at + 4 * PB], rhs_ref[total:], dims, preferred_element_type=f32)
        put(slice(step * 4, step * 4 + 4), out.reshape(4, PB, 8 * CS))


def back_own_kernel(factor_ref, h_ref, x_ref, out_ref, rhs_ref):
    def put(at, out):
        out_ref[at] = out

    back_half(factor_ref, h_ref, x_ref, rhs_ref, 0, put)


def back_other_kernel(factor_ref, h_ref, x_ref, own_ref, out_ref, rhs_ref):
    def put(at, out):
        out_ref[at] = (own_ref[at] + out).astype(bf16)

    back_half(factor_ref, h_ref, x_ref, rhs_ref, 1, put)


def back_call(kernel, name, dtype, *args):
    return pl.pallas_call(
        kernel,
        in_specs=[VMEM] * len(args),
        out_specs=VMEM,
        out_shape=jax.ShapeDtypeStruct((ROWS, PB, 8 * CS), dtype),
        scratch_shapes=[pltpu.VMEM((LS * W, 8 * CS), bf16)],
        compiler_params=params(24),
        cost_estimate=pl.CostEstimate(flops=1 << 29, bytes_accessed=4 << 20, transcendentals=0),
        name=name,
    )(*args)


def facets_kernel(parts_ref, table_ref, out_ref, buffer, sems, lhs_ref):
    steps = FP // QT
    total = parts_ref[0].astype(f32)
    for r in range(1, ROWS):
        total = total + parts_ref[r].astype(f32)
    total = total.astype(bf16)
    for a in range(2):
        for t in range(2):
            at = (a * 2 + t) * 2 * CS
            lhs_ref[(t * 2 + a) * PB : (t * 2 + a + 1) * PB, :] = total[:, at : at + 2 * CS]

    def copy(i):
        return pltpu.make_async_copy(buffer.at[i], out_ref.at[:, :, :, pl.ds(pl.multiple_of(i * QT, QT), QT)], sems.at[i])

    def body(i, carry):
        table = table_ref[:, pl.ds(pl.multiple_of(i * QT, QT), QT)]
        out = jnp.dot(lhs_ref[...], table, preferred_element_type=f32)
        buffer[i] = out.reshape(2, 2, PB, QT).astype(bf16)
        copy(i).start()
        return carry

    lax.fori_loop(0, steps, body, 0)
    for i in range(steps):
        copy(i).wait()


def facets_call(parts, table):
    steps = FP // QT
    return pl.pallas_call(
        facets_kernel,
        in_specs=[VMEM, VMEM],
        out_specs=HBM,
        out_shape=jax.ShapeDtypeStruct((2, 2, PB, FP), bf16),
        scratch_shapes=[
            pltpu.VMEM((steps, 2, 2, PB, QT), bf16),
            pltpu.SemaphoreType.DMA((steps,)),
            pltpu.VMEM((4 * PB, 2 * CS), bf16),
        ],
        compiler_params=params(24),
        cost_estimate=pl.CostEstimate(flops=2 * 256 * 128 * FP, bytes_accessed=5 << 20, transcendentals=0),
        name="facets",
    )(parts, table)


def local(facet_model, sub_offsets, tile_rows, tile_counts, visibilities):
    rows_line, grid_line, all_line = ("xh", "y"), ("zh", "zl", "sub"), ("zh", "zl", "core", "sub")
    swap = [(0, 1), (1, 0)]

    def exchange(x, axes):
        return lax.all_to_all(x, axes, split_axis=0, concat_axis=0, tiled=True)

    tiles = exchange(jnp.broadcast_to(tile_rows, (LS, TM)), all_line)
    strips = exchange(strips_call(facet_model), rows_line)
    h, live, factor, table = operator_call(tiles, sub_offsets, tile_counts, waves_call())

    other, rhs = fore_other_call(factor, h, strips)
    other = lax.ppermute(other, "core", swap)
    own = fore_own_call(factor, h, rhs)
    parts = exchange(add_call(own, other), grid_line)
    residual, back = subgrid_call(live, parts, visibilities[0])
    own = exchange(back, grid_line)
    other = lax.ppermute(own, "core", swap)
    sums = back_call(back_own_kernel, "back_own", f32, factor, h, own)
    sums = exchange(back_call(back_other_kernel, "back_other", bf16, factor, h, other, sums), rows_line)
    return facets_call(sums, table), residual[None]


def solution(mesh):
    split = Mesh(mesh.devices.reshape(4, 2, 2, 2, 4, 2), ("zh", "zl", "core", "xh", "y", "sub"))
    whole = ("zh", "zl", "core", "xh", "y", "sub")
    model = P(None, "sub", ("zh", "zl", "core", "xh", "y"), None)
    return jax.shard_map(
        local,
        mesh=split,
        in_specs=(model, P(), P(whole, None), P(whole), P(whole, None, None, None, None)),
        out_specs=(model, P(whole, None, None, None, None)),
        check_vma=False,
    )
```

```python
import math

import jax
import jax.numpy as jnp
from jax import lax
from jax.experimental import pallas as pl
from jax.experimental.pallas import tpu as pltpu
from jax.sharding import Mesh
from jax.sharding import PartitionSpec as P

SKY = 65536
FP = 8192
CS = 64
SG = 128
TM = 4
TR = 8
CH = 32
W = TM * TR
PB = 64
ROWS = 8
LP = ROWS * PB
LS = 32
QT = 1024

f32 = jnp.float32
bf16 = jnp.bfloat16


def turn(index, period):
    quarter = period // 4
    quadrant = lax.shift_right_logical(index + quarter // 2, quarter.bit_length() - 1)
    x = (index - quadrant * quarter).astype(f32) * (2.0 * math.pi / period)
    y = x * x
    sine = x * (1.0 + y * (-1.0 / 6 + y * (1.0 / 120 + y * (-1.0 / 5040 + y * (1.0 / 362880)))))
    cosine = 1.0 + y * (-0.5 + y * (1.0 / 24 + y * (-1.0 / 720 + y * (1.0 / 40320 - y * (1.0 / 3628800)))))
    swap = (quadrant & 1) == 1
    first = jnp.where(swap, sine, cosine)
    second = jnp.where(swap, cosine, sine)
    first = jnp.where(((quadrant + 1) & 2) == 2, -first, first)
    second = jnp.where((quadrant & 2) == 2, -second, second)
    return first, second


def taper(place):
    cosine, _ = turn(2 * place + 1, 2 * FP)
    return 0.625 - 0.375 * cosine


def iota(shape, dim):
    return lax.broadcasted_iota(jnp.int32, shape, dim)


def column_start(base_ref):
    place = iota((8, QT), 1)
    line = iota((8, QT), 0)
    tables = turn((line * place) & (QT - 1), QT) + turn((line * place) & (FP - 1), FP) + turn(2 * place + 1, 2 * FP)
    for i, table in enumerate(tables):
        base_ref[i] = table


def column_block(base_ref, step):
    wide = lambda x: jnp.concatenate([x] * (QT // 128), axis=1)
    move_re, move_im = (wide(x) for x in turn((iota((8, 128), 0) * step) & 7, 8))
    tilt_re, tilt_im = (wide(x) for x in turn(jnp.full((8, 128), step, jnp.int32), 8))
    cosine = base_ref[4] * tilt_re - base_ref[5] * tilt_im
    scale = (0.625 - 0.375 * cosine) * (1.0 / math.sqrt(FP))
    low_re = (base_ref[2] * move_re - base_ref[3] * move_im) * scale
    low_im = (base_ref[2] * move_im + base_ref[3] * move_re) * scale
    real, imag = [], []
    for k in range(8):
        re, im = base_ref[0, k : k + 1], base_ref[1, k : k + 1]
        real.append(low_re * re - low_im * im)
        imag.append(-(low_re * im + low_im * re))
    return jnp.concatenate(real + imag, axis=0).astype(bf16)


def subgrid_of(g):
    core = lax.axis_index("core")
    o, z, b = g // 16, (g // 2) % 8, g % 2
    c = core + o - 2 * core * o
    facet = z * 2 + c
    return facet * 2 + b, 2 * (facet * 8 + lax.axis_index("xh") * 4 + lax.axis_index("y")) + b


def line_rows(shape):
    z = lax.axis_index("zh") * 2 + lax.axis_index("zl")
    return (z * 2 + lax.axis_index("core")) * LP + iota(shape, 1)


def phase_table(ref):
    shape = (SG + TR, 2 * CS)
    cosine, sine = turn(iota(shape, 0) & (SG - 1), SG)
    ref[...] = jnp.where(iota(shape, 1) < CS, cosine, sine)


def factors(ref, step):
    x = ref[step * 8 * W : (step + 1) * 8 * W, :].astype(f32)
    y = pltpu.roll(x, CS, 1)
    left = iota(x.shape, 1) < CS
    real = jnp.where(left, x, y)
    imag = jnp.where(left, -y, x)
    return jnp.concatenate([real, real], axis=1), jnp.concatenate([imag, imag], axis=1)


def swapped(x):
    return jnp.concatenate([pltpu.roll(x[:, i : i + 2 * CS], CS, 1) for i in range(0, x.shape[1], 2 * CS)], axis=1)


SMEM = pl.BlockSpec(memory_space=pltpu.SMEM)
VMEM = pl.BlockSpec(memory_space=pltpu.VMEM)
HBM = pl.BlockSpec(memory_space=pltpu.HBM)


def params(mib):
    return pltpu.CompilerParams(vmem_limit_bytes=mib << 20)


def strips_kernel(model_ref, out_ref, buffer, sems, base_ref, table_ref):
    rows = PB // 2

    def copy(i):
        return pltpu.make_async_copy(
            model_ref.at[i // 4, (i // 2) % 2, pl.ds((i % 2) * rows, rows), :], buffer.at[i], sems.at[i]
        )

    for i in range(8):
        copy(i).start()
    column_start(base_ref)

    def body(i, carry):
        table_ref[:, pl.ds(pl.multiple_of(i * QT, QT), QT)] = column_block(base_ref, i)
        return carry

    lax.fori_loop(0, FP // QT, body, 0)
    for i in range(8):
        copy(i).wait()
    strips = lax.dot_general(
        buffer[...].reshape(4 * PB, FP), table_ref[...], (((1,), (1,)), ((), ())), preferred_element_type=f32
    ).astype(bf16)
    parts = [strips[(t * 2 + a) * PB : (t * 2 + a + 1) * PB] for a in range(2) for t in range(2)]
    strip = jnp.concatenate(parts, axis=1)
    for r in range(ROWS):
        out_ref[r] = strip


def strips_call(model):
    return pl.pallas_call(
        strips_kernel,
        in_specs=[HBM],
        out_specs=VMEM,
        out_shape=jax.ShapeDtypeStruct((ROWS, PB, 8 * CS), bf16),
        scratch_shapes=[
            pltpu.VMEM((8, PB // 2, FP), bf16),
            pltpu.SemaphoreType.DMA((8,)),
            pltpu.VMEM((6, 8, QT), f32),
            pltpu.VMEM((2 * CS, FP), bf16),
        ],
        compiler_params=params(60),
        cost_estimate=pl.CostEstimate(flops=2 * 256 * 128 * FP, bytes_accessed=5 << 20, transcendentals=0),
        name="strips",
    )(model)


def grid_table():
    l = iota((2 * CS, SG), 0) & (CS - 1)
    upper = iota((2 * CS, SG), 0) < CS
    v = iota((2 * CS, SG), 1)
    rows = []
    for b in range(2):
        cosine, sine = turn((v * (2 * l + b)) & (SG - 1), SG)
        real = jnp.where(upper, cosine, -sine)
        imag = jnp.where(upper, sine, cosine)
        rows.append(jnp.concatenate([real, imag], axis=1))
    return (jnp.concatenate(rows, axis=0) * (1.0 / math.sqrt(SG))).astype(bf16)


def waves_kernel(d_ref):
    p = line_rows((TR, LP))
    line = iota((TR, LP), 0)

    def body(i, carry):
        n = (SG * (i * TR + line) - p) & (FP - 1)
        _, under = turn(n, 2 * FP)
        _, over = turn((CS * n) & (2 * FP - 1), 2 * FP)
        ratio = jnp.where(n == 0, float(CS), over / jnp.where(n == 0, 1.0, under))
        re, im = turn(((CS - 1) * n) & (2 * FP - 1), 2 * FP)
        for c, part in enumerate((re * ratio, im * ratio)):
            for q in range(LP // 128):
                d_ref[c, q, pl.ds(pl.multiple_of(i * TR, TR), TR), :] = part[:, q * 128 : (q + 1) * 128]
        return carry

    lax.fori_loop(0, SG // TR, body, 0)


def waves_call():
    return pl.pallas_call(
        waves_kernel,
        out_specs=VMEM,
        out_shape=jax.ShapeDtypeStruct((2, LP // 128, SG, 128), f32),
        compiler_params=params(24),
        cost_estimate=pl.CostEstimate(flops=8 << 20, bytes_accessed=1 << 20, transcendentals=0),
        name="waves",
    )()


def operator_kernel(
    tiles_ref, offsets_ref, count_ref, d_ref, h_ref, live_ref, factor_ref, grid_ref, table_ref, e_ref, phase_ref, buffer, sems, base_ref
):
    def copy(i):
        return pltpu.make_async_copy(buffer.at[i], table_ref.at[:, pl.ds(pl.multiple_of(i * QT, QT), QT)], sems.at[i])

    def block(i, carry):
        buffer[i] = column_block(base_ref, i)
        copy(i).start()
        return carry

    column_start(base_ref)
    lax.fori_loop(0, FP // QT, block, 0)
    phase_table(phase_ref)
    grid_ref[...] = grid_table()
    live_ref[...] = jnp.where(iota((W, 128), 0) < TR * count_ref[0], 1.0, 0.0)
    place = line_rows((8, LP))
    line = iota((8, LP), 0)
    scale = taper(place) * (1.0 / 1024)

    def body(step, carry):
        offset = jnp.zeros((8, LP), jnp.int32)
        index, offs = [], []
        for i in range(8):
            at, s = subgrid_of(step * 8 + i)
            index.append(at)
            offs.append(offsets_ref[s])
            offset = jnp.where(line == i, offsets_ref[s], offset)
        cosine, sine = turn((offset * place) & (SKY - 1), SKY)
        e_ref[0] = cosine * scale
        e_ref[1] = -sine * scale
        for half in range(2):
            real, imag, factor = [], [], []
            for i in range(4 * half, 4 * half + 4):
                er = e_ref[0, i : i + 1, :]
                ei = e_ref[1, i : i + 1, :]
                for j in range(TM):
                    at = tiles_ref[index[i], j]
                    n = (at - 16 * offs[i]) & (SG - 1)
                    factor.append(phase_ref[pl.ds(n, TR), :])
                    dr = jnp.concatenate([d_ref[0, q, pl.ds(at, TR), :] for q in range(LP // 128)], axis=1)
                    di = jnp.concatenate([d_ref[1, q, pl.ds(at, TR), :] for q in range(LP // 128)], axis=1)
                    real.append(dr * er - di * ei)
                    imag.append(dr * ei + di * er)
            rows = pl.ds(pl.multiple_of(step * 8 * W + half * 4 * W, 4 * W), 4 * W)
            h_ref[rows, :LP] = jnp.concatenate(real, axis=0).astype(bf16)
            h_ref[rows, LP:] = jnp.concatenate(imag, axis=0).astype(bf16)
            factor_ref[rows, :] = jnp.concatenate(factor, axis=0).astype(bf16)
        return carry

    lax.fori_loop(0, LS // 8, body, 0)
    for i in range(FP // QT):
        copy(i).wait()


def operator_call(tiles, offsets, count, waves):
    return pl.pallas_call(
        operator_kernel,
        in_specs=[SMEM, SMEM, SMEM, VMEM],
        out_specs=[VMEM, VMEM, VMEM, VMEM, HBM],
        out_shape=[
            jax.ShapeDtypeStruct((LS * W, 2 * LP), bf16),
            jax.ShapeDtypeStruct((W, 128), f32),
            jax.ShapeDtypeStruct((LS * W, 2 * CS), bf16),
            jax.ShapeDtypeStruct((4 * CS, 2 * SG), bf16),
            pltpu.HBM((2 * CS, FP), bf16),
        ],
        scratch_shapes=[
            pltpu.VMEM((2, 8, LP), f32),
            pltpu.VMEM((SG + TR, 2 * CS), f32),
            pltpu.VMEM((FP // QT, 2 * CS, QT), bf16),
            pltpu.SemaphoreType.DMA((FP // QT,)),
            pltpu.VMEM((6, 8, QT), f32),
        ],
        compiler_params=params(24),
        cost_estimate=pl.CostEstimate(flops=20 << 20, bytes_accessed=8 << 20, transcendentals=0),
        name="operator",
    )(tiles, offsets, count, waves)


HALF = jax.ShapeDtypeStruct((LS // 2, W, 4 * CS), bf16)


def fore_half(factor_ref, h_ref, rhs_ref, o, put):
    rows = 8 * W
    for q in range(2):
        step = 2 * o + q
        out = jnp.dot(h_ref[step * rows : (step + 1) * rows, :], rhs_ref[...], preferred_element_type=f32)
        real, imag = factors(factor_ref, step)
        second = out[:, 4 * CS :]
        out = out[:, : 4 * CS] + second * real + swapped(second) * imag
        put(slice(q * 8, q * 8 + 8), out.reshape(8, W, 4 * CS))


def fore_other_kernel(factor_ref, h_ref, strips_ref, out_ref, rhs_ref):
    left = iota((PB, 2 * CS), 1) < CS
    for r in range(ROWS):
        strips = strips_ref[r]
        rhs_ref[r * PB : (r + 1) * PB, :] = strips
        for at in range(0, 8 * CS, 2 * CS):
            turned = pltpu.roll(strips[:, at : at + 2 * CS].astype(f32), CS, 1)
            rhs_ref[LP + r * PB : LP + (r + 1) * PB, at : at + 2 * CS] = jnp.where(left, -turned, turned).astype(bf16)

    def put(at, out):
        out_ref[at] = out.astype(bf16)

    fore_half(factor_ref, h_ref, rhs_ref, 1, put)


def fore_own_kernel(factor_ref, h_ref, rhs_ref, out_ref):
    def put(at, out):
        out_ref[at] = out.astype(bf16)

    fore_half(factor_ref, h_ref, rhs_ref, 0, put)


def fore_other_call(factor, h, strips):
    return pl.pallas_call(
        fore_other_kernel,
        in_specs=[VMEM, VMEM, VMEM],
        out_specs=[VMEM, VMEM],
        out_shape=[HALF, jax.ShapeDtypeStruct((2 * LP, 8 * CS), bf16)],
        compiler_params=params(24),
        cost_estimate=pl.CostEstimate(flops=1 << 29, bytes_accessed=4 << 20, transcendentals=0),
        name="fore_other",
    )(factor, h, strips)


def fore_own_call(factor, h, rhs):
    return pl.pallas_call(
        fore_own_kernel,
        in_specs=[VMEM, VMEM, VMEM],
        out_specs=VMEM,
        out_shape=HALF,
        compiler_params=params(24),
        cost_estimate=pl.CostEstimate(flops=1 << 29, bytes_accessed=4 << 20, transcendentals=0),
        name="fore_own",
    )(factor, h, rhs)


def add_kernel(own_ref, other_ref, out_ref):
    out_ref[...] = (own_ref[...].astype(f32) + other_ref[...].astype(f32)).astype(bf16)


def add_call(own, other):
    return pl.pallas_call(
        add_kernel,
        in_specs=[VMEM, VMEM],
        out_specs=VMEM,
        out_shape=jax.ShapeDtypeStruct(own.shape, bf16),
        compiler_params=params(24),
        cost_estimate=pl.CostEstimate(flops=1 << 18, bytes_accessed=1 << 20, transcendentals=0),
        name="add",
    )(own, other)


def subgrid_kernel(live_ref, grid_ref, parts_ref, vis_ref, res_ref, out_ref, buffer, sems):
    table = grid_ref[...]
    fronts = []
    for b in range(2):
        total = parts_ref[b].astype(f32)
        for z in range(1, 8):
            total = total + parts_ref[2 * z + b].astype(f32)
        fronts.append(total.astype(bf16))
    front = jnp.concatenate(
        [jnp.concatenate([fronts[b][:, t * 2 * CS : (t + 1) * 2 * CS] for b in range(2)], axis=1) for t in range(2)],
        axis=0,
    )
    sky = jnp.dot(front, table, preferred_element_type=f32).astype(bf16).astype(f32)
    weighted = [[], []]
    for j in range(TM):
        m0 = sky[j * TR : (j + 1) * TR]
        m1 = sky[W + j * TR : W + (j + 1) * TR]
        live = live_ref[j * TR : (j + 1) * TR, :]
        live = jnp.concatenate([live, live], axis=1)
        w0 = jnp.zeros((TR, 2 * SG), f32)
        w1 = jnp.zeros((TR, 2 * SG), f32)
        for c in range(CH):
            nu = (c + 0.5) / CH - 0.5
            res = (vis_ref[j, c].astype(f32) - (m0 + nu * m1)) * live
            buffer[j, c] = res.astype(bf16)
            w0 = w0 + res
            w1 = w1 + nu * res
        pltpu.make_async_copy(buffer.at[j], res_ref.at[j], sems.at[j]).start()
        weighted[0].append(w0)
        weighted[1].append(w1)
    weight = jnp.concatenate(weighted[0] + weighted[1], axis=0).astype(bf16)
    back = lax.dot_general(weight, table, (((1,), (1,)), ((), ())), preferred_element_type=f32).astype(bf16)
    for b in range(2):
        block = jnp.concatenate([back[t * W : (t + 1) * W, b * 2 * CS : (b + 1) * 2 * CS] for t in range(2)], axis=1)
        for z in range(8):
            out_ref[2 * z + b] = block
    for j in range(TM):
        pltpu.make_async_copy(buffer.at[j], res_ref.at[j], sems.at[j]).wait()


def subgrid_call(live, grid, parts, vis):
    return pl.pallas_call(
        subgrid_kernel,
        in_specs=[VMEM, VMEM, VMEM, VMEM],
        out_specs=[HBM, VMEM],
        out_shape=[
            jax.ShapeDtypeStruct((TM, CH, TR, 2 * SG), bf16),
            jax.ShapeDtypeStruct((LS // 2, W, 4 * CS), bf16),
        ],
        scratch_shapes=[pltpu.VMEM((TM, CH, TR, 2 * SG), bf16), pltpu.SemaphoreType.DMA((TM,))],
        compiler_params=params(24),
        cost_estimate=pl.CostEstimate(flops=20 << 20, bytes_accessed=2 << 20, transcendentals=0),
        name="subgrid",
    )(live, grid, parts, vis)


def back_half(factor_ref, h_ref, x_ref, rhs_ref, o, put):
    left = (iota((8 * W, 8 * CS), 1) & (2 * CS - 1)) < CS
    total = LS * W // 2
    for q in range(2):
        x = x_ref[q * 8 : q * 8 + 8].reshape(8 * W, 4 * CS).astype(f32)
        y = swapped(x)
        real, imag = factors(factor_ref, 2 * o + q)
        both = jnp.concatenate([x, x * real - y * imag], axis=1)
        turned = jnp.concatenate([y, y * real + x * imag], axis=1)
        rhs_ref[q * 8 * W : (q + 1) * 8 * W, :] = both.astype(bf16)
        rhs_ref[total + q * 8 * W : total + (q + 1) * 8 * W, :] = jnp.where(left, turned, -turned).astype(bf16)
    dims = (((0,), (0,)), ((), ()))
    rows = slice(o * total, (o + 1) * total)
    for step in range(2):
        at = step * 4 * PB
        out = lax.dot_general(h_ref[rows, at : at + 4 * PB], rhs_ref[:total], dims, preferred_element_type=f32)
        out = out + lax.dot_general(h_ref[rows, LP + at : LP + at + 4 * PB], rhs_ref[total:], dims, preferred_element_type=f32)
        put(slice(step * 4, step * 4 + 4), out.reshape(4, PB, 8 * CS))


def back_own_kernel(factor_ref, h_ref, x_ref, out_ref, rhs_ref):
    def put(at, out):
        out_ref[at] = out

    back_half(factor_ref, h_ref, x_ref, rhs_ref, 0, put)


def back_other_kernel(factor_ref, h_ref, x_ref, own_ref, out_ref, rhs_ref):
    def put(at, out):
        out_ref[at] = (own_ref[at] + out).astype(bf16)

    back_half(factor_ref, h_ref, x_ref, rhs_ref, 1, put)


def back_call(kernel, name, dtype, *args):
    return pl.pallas_call(
        kernel,
        in_specs=[VMEM] * len(args),
        out_specs=VMEM,
        out_shape=jax.ShapeDtypeStruct((ROWS, PB, 8 * CS), dtype),
        scratch_shapes=[pltpu.VMEM((LS * W, 8 * CS), bf16)],
        compiler_params=params(24),
        cost_estimate=pl.CostEstimate(flops=1 << 29, bytes_accessed=4 << 20, transcendentals=0),
        name=name,
    )(*args)


def facets_kernel(parts_ref, table_ref, out_ref, buffer, sems, lhs_ref):
    steps = FP // QT
    total = parts_ref[0].astype(f32)
    for r in range(1, ROWS):
        total = total + parts_ref[r].astype(f32)
    total = total.astype(bf16)
    for a in range(2):
        for t in range(2):
            at = (a * 2 + t) * 2 * CS
            lhs_ref[(t * 2 + a) * PB : (t * 2 + a + 1) * PB, :] = total[:, at : at + 2 * CS]

    def copy(i):
        return pltpu.make_async_copy(buffer.at[i], out_ref.at[:, :, :, pl.ds(pl.multiple_of(i * QT, QT), QT)], sems.at[i])

    def body(i, carry):
        table = table_ref[:, pl.ds(pl.multiple_of(i * QT, QT), QT)]
        out = jnp.dot(lhs_ref[...], table, preferred_element_type=f32)
        buffer[i] = out.reshape(2, 2, PB, QT).astype(bf16)
        copy(i).start()
        return carry

    lax.fori_loop(0, steps, body, 0)
    for i in range(steps):
        copy(i).wait()


def facets_call(parts, table):
    steps = FP // QT
    return pl.pallas_call(
        facets_kernel,
        in_specs=[VMEM, VMEM],
        out_specs=HBM,
        out_shape=jax.ShapeDtypeStruct((2, 2, PB, FP), bf16),
        scratch_shapes=[
            pltpu.VMEM((steps, 2, 2, PB, QT), bf16),
            pltpu.SemaphoreType.DMA((steps,)),
            pltpu.VMEM((4 * PB, 2 * CS), bf16),
        ],
        compiler_params=params(24),
        cost_estimate=pl.CostEstimate(flops=2 * 256 * 128 * FP, bytes_accessed=5 << 20, transcendentals=0),
        name="facets",
    )(parts, table)


def local(facet_model, sub_offsets, tile_rows, tile_counts, visibilities):
    rows_line, grid_line, all_line = ("xh", "y"), ("zh", "zl", "sub"), ("zh", "zl", "core", "sub")
    swap = [(0, 1), (1, 0)]

    def exchange(x, axes):
        return lax.all_to_all(x, axes, split_axis=0, concat_axis=0, tiled=True)

    tiles = exchange(jnp.broadcast_to(tile_rows, (LS, TM)), all_line)
    strips = exchange(strips_call(facet_model), rows_line)
    h, live, factor, grid, table = operator_call(tiles, sub_offsets, tile_counts, waves_call())

    other, rhs = fore_other_call(factor, h, strips)
    other = lax.ppermute(other, "core", swap)
    own = fore_own_call(factor, h, rhs)
    parts = exchange(add_call(own, other), grid_line)
    residual, back = subgrid_call(live, grid, parts, visibilities[0])
    own = exchange(back, grid_line)
    other = lax.ppermute(own, "core", swap)
    sums = back_call(back_own_kernel, "back_own", f32, factor, h, own)
    sums = exchange(back_call(back_other_kernel, "back_other", bf16, factor, h, other, sums), rows_line)
    return facets_call(sums, table), residual[None]


def solution(mesh):
    split = Mesh(mesh.devices.reshape(4, 2, 2, 2, 4, 2), ("zh", "zl", "core", "xh", "y", "sub"))
    whole = ("zh", "zl", "core", "xh", "y", "sub")
    model = P(None, "sub", ("zh", "zl", "core", "xh", "y"), None)
    return jax.shard_map(
        local,
        mesh=split,
        in_specs=(model, P(), P(whole, None), P(whole), P(whole, None, None, None, None)),
        out_specs=(model, P(whole, None, None, None, None)),
        check_vma=False,
    )
```
